768 devices in a mesh: height: 96 (over y, z_lo, core), dp: 8 (over z_hi, x).
Axes of the slice: x: 4, y: 8, z: 12 (z_hi: 2, z_lo: 6; z = z_hi * 6 + z_lo), core: 2. Of those that a mesh axis runs over, the one named last changes fastest.
Arguments:
- x_next: bfloat16 [8, 192, 320, 128], P('dp', 'height'), may hold values from -12 to 12
- x_cur: bfloat16 [8, 192, 320, 128], P('dp', 'height'), may hold values from -12 to 12
- grad_out: bfloat16 [8, 192, 320, 128], P('dp', 'height'), may hold values from -6 to 6
- kernel: bfloat16 [3, 3, 320, 320], replicated, may hold values from -0.109375 to 0.109375
- gamma: float32 [320], replicated, may hold values from 0.25 to 1.75
- beta: float32 [320], replicated, may hold values from -2.5 to 2.5
Outputs:
- y_next: bfloat16 [8, 192, 320, 128], P('dp', 'height')
- grad_x: bfloat16 [8, 192, 320, 128], P('dp', 'height')
- grad_kernel: float32 [921600], P(('height', 'dp'))
The draws below stay inside these ranges and needn't reach their ends.
All inputs are finite; a program needn't handle non-finite values.
Results may differ from the reference program's by a relative error of at most 0.0049.
Values may be sent and summed in bfloat16 or wider, within the bound.
A program may use at most 64 MiB of HBM per device.

```python
import jax
import jax.numpy as jnp
from jax import lax

CHANNELS = 320
GROUPS = 32
COLUMNS = 128
ROWS = 192
SAMPLES = 8


def draw_inputs(key):
    key_base, key_rows, key_chan, key_offset = jax.random.split(key, 4)
    shape = (SAMPLES, ROWS, CHANNELS, COLUMNS)
    base = jax.random.normal(key_base, shape, jnp.float32)
    spread = jax.random.uniform(key_rows, (1, ROWS, 1, 1), jnp.float32, 0.7, 1.3)
    rising = (0.6 + 1.2 * jnp.arange(ROWS, dtype=jnp.float32) / ROWS).reshape(1, ROWS, 1, 1)
    channel_scale = jnp.exp(jax.random.uniform(key_chan, (SAMPLES, 1, CHANNELS, 1), jnp.float32, -0.5, 0.5))
    offset = 0.3 * jax.random.normal(key_offset, (1, ROWS, 1, 1), jnp.float32)
    values = base * spread * rising * channel_scale + offset
    return jnp.clip(values, -12.0, 12.0).astype(jnp.bfloat16)


def draw_x_next(key, part):
    return draw_inputs(jax.random.fold_in(key, 11))


def draw_x_cur(key, part):
    return draw_inputs(jax.random.fold_in(key, 12))


def levels(own_key, dims, cuts, least, top_value):
    loudness, own = 1.0, jax.random.fold_in(own_key, 6)
    for dim, parts in cuts:
        heights = jnp.exp(jax.random.uniform(jax.random.fold_in(own, dim), (parts,), jnp.float32, least / len(cuts), top_value / len(cuts)))
        loudness = loudness * jnp.repeat(heights, dims[dim] // parts).reshape([-1 if axis == dim else 1 for axis in range(len(dims))])
    return loudness


def centred(stream_key, dims, width, most, cuts=(), kind=jnp.bfloat16):
    level = levels(stream_key, dims, cuts, -0.22, 0.18) if cuts else 1.0
    array = jax.random.normal(stream_key, dims, jnp.float32) * width * level
    return jnp.minimum(jnp.maximum(array, -most), most).astype(kind)


def setup_inputs(seed: int = 0) -> dict:
    arg_keys = jax.random.split(jax.random.key(seed), 7)
    x_next = draw_x_next(jax.random.fold_in(arg_keys[6], 71), 0)
    x_cur = draw_x_cur(jax.random.fold_in(arg_keys[6], 71), 0)
    grad_out = centred(arg_keys[2], (SAMPLES, ROWS, CHANNELS, COLUMNS), 1.0, 6.0, ((0, 8), (1, 96)))
    kernel = centred(arg_keys[3], (3, 3, CHANNELS, CHANNELS), (9 * CHANNELS) ** -0.5, 0.109375)
    gamma = jnp.clip(1.0 + 0.15 * jax.random.normal(arg_keys[4], (CHANNELS,), jnp.float32), 0.25, 1.75)
    beta = centred(arg_keys[5], (CHANNELS,), 0.5, 2.5, (), jnp.float32)
    return dict(x_next=x_next, x_cur=x_cur, grad_out=grad_out, kernel=kernel, gamma=gamma, beta=beta)


eps = 1e-05

def conv_full(image, weights):
    padded = jnp.pad(image, ((1, 1), (0, 0), (1, 1)))
    total = jnp.zeros((image.shape[0], weights.shape[2], image.shape[2]), jnp.float32)
    for tap_row in range(3):
        for tap_col in range(3):
            window = padded[tap_row:tap_row + image.shape[0], :, tap_col:tap_col + image.shape[2]]
            total = total + jnp.einsum('oc,hcw->how', weights[tap_row, tap_col], window)
    return total

def group_stats(value):
    grouped = value.reshape(value.shape[0], GROUPS, CHANNELS // GROUPS, value.shape[2])
    center = lax.optimization_barrier(jnp.mean(grouped, axis=(0, 2, 3), keepdims=True))
    spread = lax.optimization_barrier(jnp.mean((grouped - center) ** 2, axis=(0, 2, 3), keepdims=True))
    return (center, lax.rsqrt(spread + eps))

def normalize(value, gamma, beta):
    center, scale_inv = group_stats(value)
    grouped = value.reshape(value.shape[0], GROUPS, CHANNELS // GROUPS, value.shape[2])
    normed = ((grouped - center) * scale_inv).reshape(value.shape)
    affine = normed * gamma[None, :, None] + beta[None, :, None]
    return (normed, affine, scale_inv)

def one_sample(weights, gamma, beta, inputs):
    x_next, x_cur, grad_out = inputs
    z_next = conv_full(x_next.astype(jnp.float32), weights)
    normed, affine, scale_inv = normalize(z_next, gamma, beta)
    y_next = (affine * jax.nn.sigmoid(affine)).astype(jnp.bfloat16)
    x_float = x_cur.astype(jnp.float32)
    z_cur = conv_full(x_float, weights)
    normed, affine, scale_inv = normalize(z_cur, gamma, beta)
    sig = jax.nn.sigmoid(affine)
    grad_a = grad_out.astype(jnp.float32) * (sig * (1.0 + affine * (1.0 - sig)))
    grad_n = grad_a * gamma[None, :, None]
    shape = (z_cur.shape[0], GROUPS, CHANNELS // GROUPS, z_cur.shape[2])
    gn_grouped = grad_n.reshape(shape)
    n_grouped = normed.reshape(shape)
    first_mean = lax.optimization_barrier(jnp.mean(gn_grouped, axis=(0, 2, 3), keepdims=True))
    second_mean = lax.optimization_barrier(jnp.mean(gn_grouped * n_grouped, axis=(0, 2, 3), keepdims=True))
    grad_z = (scale_inv * (gn_grouped - first_mean - n_grouped * second_mean)).reshape(z_cur.shape)
    grad_z = grad_z.astype(jnp.bfloat16).astype(jnp.float32)
    primal, pullback = jax.vjp(conv_full, x_float, weights)
    grad_input, grad_weights = pullback(grad_z)
    return (y_next, grad_input.astype(jnp.bfloat16), grad_weights)

def reference(x_next, x_cur, grad_out, kernel, gamma, beta):
    weights = kernel.astype(jnp.float32)
    y_next, grad_x, per_sample = lax.map(lambda item: one_sample(weights, gamma, beta, item), (x_next, x_cur, grad_out))
    return (y_next, grad_x, lax.optimization_barrier(jnp.sum(per_sample, axis=0)).reshape(-1))
```

```python
import jax
import jax.numpy as jnp
from jax import lax
from jax.experimental import pallas as pl
from jax.experimental.pallas import tpu as pltpu
from jax.sharding import Mesh
from jax.sharding import PartitionSpec as P

CH = 320
COLS = 128
PAD = 384
GROUP = 10
NY, NZL, NC, NZH, NX = 8, 6, 2, 2, 4
NM = NZL * NC
NH = NY * NM
NZ = NZL * NZH
COUNT = 192 * GROUP * COLS
EPS = 1e-05
HEIGHT = ("y", "zl", "core")
DP = ("zh", "x")
FIRST = (0, 10, 21)
BLOCKS = (11, 12, 11)
ORDER = (0, 3, 1, 4, 2, 5)

f32 = jnp.float32
bf16 = jnp.bfloat16


def dot(a, b, dims=(((1,), (0,)), ((), ()))):
    return lax.dot_general(a, b, dims, preferred_element_type=f32)


NT = (((1,), (1,)), ((), ()))
TN = (((0,), (0,)), ((), ()))


def body(
    xn_in, xc_in, go_in, k_in, gam_in, bet_in,
    y_out, gx_out, gk_out,
    xcr, xnr, gor, kv, xcs, xns, gzo, gzh, gzs,
    zc, zn, nrm, gn, emask, gam, bet, selm,
    ra, rb, ra2, rb2,
    gacc, s1, r1, s2, r2, s3, r3, s4, r4, bown, s5, cown, r5, r6,
    lsem, hs, hr, ghs, ghr, as_, ar, bs, br, as2, ar2, bs2, br2,
    c1s, c1r, c2s, c2r, c3s, c3r, c4s, c4r, c5s, c5r, c6s, c6r,
):
    yy, zl, co = lax.axis_index("y"), lax.axis_index("zl"), lax.axis_index("core")
    zh, xx = lax.axis_index("zh"), lax.axis_index("x")
    m = zl * NC + co
    pos = yy * NM + m
    z12 = zl * NZH + zh

    def height_id(p):
        return {"y": p // NM, "zl": (p // NC) % NZL, "core": p % NC}

    has_prev, has_next = pos > 0, pos < NH - 1
    prev_id, next_id = height_id(jnp.maximum(pos - 1, 0)), height_id(jnp.minimum(pos + 1, NH - 1))

    cp_xc = pltpu.make_async_copy(xc_in.at[0], xcr.at[pl.ds(1, 2)], lsem.at[0])
    cp_k = pltpu.make_async_copy(k_in, kv, lsem.at[1])
    cp_xn = pltpu.make_async_copy(xn_in.at[0], xnr.at[pl.ds(1, 2)], lsem.at[2])
    cp_go = pltpu.make_async_copy(go_in.at[0], gor, lsem.at[3])
    for cp in (cp_xc, cp_k, cp_xn, cp_go):
        cp.start()

    barrier = pltpu.get_barrier_semaphore()

    def greet(device_id):
        pl.semaphore_signal(barrier, inc=1, device_id=device_id, device_id_type=pl.DeviceIdType.MESH)

    @pl.when(has_prev)
    def _():
        greet(prev_id)

    @pl.when(has_next)
    def _():
        greet(next_id)

    def far_z(i, c):
        greet({"zl": i, "zh": 1 - zh})
        return c

    lax.fori_loop(0, NZL, far_z, 0)

    def far_m(i, c):
        t = (m + i) % NM
        greet({"zl": t // NC, "core": t % NC})
        return c

    lax.fori_loop(1, NM, far_m, 0)

    def far_y(i, c):
        greet({"y": (yy + i) % NY})
        return c

    lax.fori_loop(1, NY, far_y, 0)

    def far_x(i, c):
        greet({"x": (xx + i) % NX})
        return c

    lax.fori_loop(1, NX, far_x, 0)

    rows_i = lax.broadcasted_iota(jnp.int32, (CH, COLS), 0)
    lane_i = lax.broadcasted_iota(jnp.int32, (CH, COLS), 1)
    rel = rows_i - GROUP * (lane_i & 31)
    emask[...] = jnp.where((rel >= 0) & (rel < GROUP), 1.0, 0.0).astype(f32)
    eye = lax.broadcasted_iota(jnp.int32, (CH, CH), 0) == lax.broadcasted_iota(jnp.int32, (CH, CH), 1)
    gam[...] = jnp.sum(jnp.where(eye, gam_in[...], 0.0), axis=1, keepdims=True)
    bet[...] = jnp.sum(jnp.where(eye, bet_in[...], 0.0), axis=1, keepdims=True)
    zc[...] = jnp.zeros_like(zc)
    zn[...] = jnp.zeros_like(zn)
    for b in range(3):
        for r in range(4):
            xcs[b, r, CH:, :] = jnp.zeros((PAD - CH, COLS), bf16)

    lane = lax.broadcasted_iota(jnp.int32, (CH, COLS), 1)

    def put_shifts(dst, row, v):
        wide = v.astype(f32)
        dst[0, row, :CH, :] = jnp.where(lane == 0, 0.0, pltpu.roll(wide, 1, 1)).astype(bf16)
        dst[1, row, :CH, :] = v
        dst[2, row, :CH, :] = jnp.where(lane == COLS - 1, 0.0, pltpu.roll(wide, COLS - 1, 1)).astype(bf16)

    cp_xc.wait()
    put_shifts(xcs, 1, xcr[1])
    put_shifts(xcs, 2, xcr[2])

    core27 = NZL + (NM - 1) + (NY - 1) + (NX - 1)
    pl.semaphore_wait(barrier, core27 + has_prev.astype(jnp.int32) + has_next.astype(jnp.int32))

    def halo(src, dst, to_next, i, send, recv):
        return pltpu.make_async_remote_copy(
            src_ref=src.at[0, 1] if to_next else src.at[0, 0],
            dst_ref=dst.at[0] if to_next else dst.at[3],
            send_sem=send.at[i],
            recv_sem=recv.at[i],
            device_id=next_id if to_next else prev_id,
            device_id_type=pl.DeviceIdType.MESH,
        )

    halos = (
        halo(xc_in, xcr, True, 0, hs, hr),
        halo(xc_in, xcr, False, 1, hs, hr),
        halo(xn_in, xnr, True, 2, hs, hr),
        halo(xn_in, xnr, False, 3, hs, hr),
    )

    @pl.when(has_next)
    def _():
        halos[0].start()

    @pl.when(has_prev)
    def _():
        halos[1].start()

    @pl.when(has_next)
    def _():
        halos[2].start()

    @pl.when(has_prev)
    def _():
        halos[3].start()

    cp_k.wait()

    def inner(b, c):
        x1, x2 = xcs[b, 1, :CH], xcs[b, 2, :CH]
        zc[...] += dot(kv[1, b], jnp.concatenate([x1, x2], axis=1))
        zc[:, COLS:] += dot(kv[0, b], x1)
        zc[:, :COLS] += dot(kv[2, b], x2)
        return c

    lax.fori_loop(0, 3, inner, 0)

    for b in range(3):
        n = BLOCKS[b] * 32
        rho = lax.broadcasted_iota(jnp.int32, (n, CH), 0)
        col = lax.broadcasted_iota(jnp.int32, (n, CH), 1)
        part = ((rho >> 3) & 3) * 4 + (rho & 3)
        src = 30 * (FIRST[b] + (rho >> 5)) + 15 * ((rho >> 2) & 1) + part - CH * b
        selm[b, :n, :] = jnp.where((part < 15) & (src == col), 1.0, 0.0).astype(bf16)

    def halo_wait(raw, shifted, up, down):
        @pl.when(has_prev)
        def _():
            up.wait_recv()

        @pl.when(jnp.logical_not(has_prev))
        def _():
            raw[0] = jnp.zeros((CH, COLS), bf16)

        @pl.when(has_next)
        def _():
            down.wait_recv()

        @pl.when(jnp.logical_not(has_next))
        def _():
            raw[3] = jnp.zeros((CH, COLS), bf16)

        put_shifts(shifted, 0, raw[0])
        put_shifts(shifted, 3, raw[3])

    halo_wait(xcr, xcs, halos[0], halos[1])

    def outer(b, c):
        zc[:, :COLS] += dot(kv[0, b], xcs[b, 0, :CH])
        zc[:, COLS:] += dot(kv[2, b], xcs[b, 3, :CH])
        return c

    lax.fori_loop(0, 3, outer, 0)

    def tile_of(cols4):
        q = lane >> 5
        picked = jnp.zeros((CH, COLS), f32)
        for i, v in enumerate(cols4):
            picked = jnp.where(q == i, v, picked)
        return jnp.sum((picked * emask[...]).reshape(CH // 8, 8, COLS), axis=0)

    def a_copy(buf, send, recv, i, slot, t):
        return pltpu.make_async_remote_copy(
            src_ref=buf.at[slot],
            dst_ref=buf.at[slot],
            send_sem=send.at[i],
            recv_sem=recv.at[slot],
            device_id={"zl": t // NC, "core": t % NC},
            device_id_type=pl.DeviceIdType.MESH,
        )

    def b_copy(buf, send, recv, i, slot, t):
        return pltpu.make_async_remote_copy(
            src_ref=buf.at[slot],
            dst_ref=buf.at[slot],
            send_sem=send.at[i],
            recv_sem=recv.at[slot],
            device_id={"y": t},
            device_id_type=pl.DeviceIdType.MESH,
        )

    def start_all(copy, buf, send, recv, me, n, tile):
        buf[me] = tile

        def go(i, c):
            copy(buf, send, recv, i, me, (me + i) % n).start()
            return c

        lax.fori_loop(1, n, go, 0)

    def wait_all(copy, buf, send, recv, me, n):
        def go(i, c):
            t = (me + i) % n
            copy(buf, send, recv, i, t, t).wait_recv()
            return c

        lax.fori_loop(1, n, go, 0)
        return jnp.sum(buf[...], axis=0)

    def sent_all(copy, buf, send, recv, me, n):
        def go(i, c):
            copy(buf, send, recv, i, me, (me + i) % n).wait_send()
            return c

        lax.fori_loop(1, n, go, 0)

    z = zc[...]
    start_all(
        a_copy, ra, as_, ar, m, NM,
        tile_of((jnp.sum(z, axis=1, keepdims=True), jnp.sum(z * z, axis=1, keepdims=True))),
    )

    cp_xn.wait()
    put_shifts(xns, 1, xnr[1])
    put_shifts(xns, 2, xnr[2])
    halo_wait(xnr, xns, halos[2], halos[3])

    def whole(t, c):
        a, b = t // 3, t % 3
        zn[...] += dot(
            kv[a, b], jnp.concatenate([xns[b, a, :CH], xns[b, a + 1, :CH]], axis=1)
        )
        return c

    lax.fori_loop(0, 5, whole, 0)
    start_all(b_copy, rb, bs, br, yy, NY, wait_all(a_copy, ra, as_, ar, m, NM))
    lax.fori_loop(5, 9, whole, 0)
    zv = zn[...]
    next_sums = (jnp.sum(zv, axis=1, keepdims=True), jnp.sum(zv * zv, axis=1, keepdims=True))
    cp_go.wait()
    total = wait_all(b_copy, rb, bs, br, yy, NY)

    def column(row, block):
        keep = (lane >> 5) == block
        return jnp.sum(jnp.where(keep, emask[...] * row, 0.0), axis=1, keepdims=True)

    def moments(tile, first):
        row = jnp.sum(tile, axis=0, keepdims=True) / COUNT
        mean_row = pltpu.roll(jnp.broadcast_to(row, (8, COLS)), (128 - 32 * first) % 128, 1)[:1]
        square_row = pltpu.roll(jnp.broadcast_to(row, (8, COLS)), (128 - 32 * (first + 1)) % 128, 1)[:1]
        rstd_row = lax.rsqrt(square_row - mean_row * mean_row + EPS)
        return column(mean_row, 0), column(rstd_row, 0)

    mean_c, rstd_c = moments(total, 0)
    normed = (zc[...] - mean_c) * rstd_c
    nrm[...] = normed
    affine = normed * gam[...] + bet[...]
    sig = jax.nn.sigmoid(affine)
    grad = jnp.concatenate([gor[0], gor[1]], axis=1).astype(f32)
    grad_n = grad * (sig * (1.0 + affine * (1.0 - sig))) * gam[...]
    gn[...] = grad_n
    start_all(
        a_copy, ra2, as2, ar2, m, NM,
        tile_of(
            (
                jnp.sum(grad_n, axis=1, keepdims=True),
                jnp.sum(grad_n * normed, axis=1, keepdims=True),
            )
            + next_sums
        ),
    )
    start_all(b_copy, rb2, bs2, br2, yy, NY, wait_all(a_copy, ra2, as2, ar2, m, NM))
    total2 = wait_all(b_copy, rb2, bs2, br2, yy, NY)
    row2 = jnp.sum(total2, axis=0, keepdims=True) / COUNT
    mean_1, mean_2 = column(row2, 0), column(row2, 1)
    gz = (rstd_c * (gn[...] - mean_1 - nrm[...] * mean_2)).astype(bf16)
    gzo[0] = gz[:, :COLS]
    gzo[1] = gz[:, COLS:]

    def gz_copy(to_next):
        return pltpu.make_async_remote_copy(
            src_ref=gzo.at[1] if to_next else gzo.at[0],
            dst_ref=gzh.at[0] if to_next else gzh.at[1],
            send_sem=ghs.at[0 if to_next else 1],
            recv_sem=ghr.at[0 if to_next else 1],
            device_id=next_id if to_next else prev_id,
            device_id_type=pl.DeviceIdType.MESH,
        )

    gz_next, gz_prev = gz_copy(True), gz_copy(False)

    @pl.when(has_next)
    def _():
        gz_next.start()

    @pl.when(has_prev)
    def _():
        gz_prev.start()

    picked = [dot(selm[b, : BLOCKS[b] * 32], gz).astype(bf16) for b in range(3)]
    for a in range(3):
        for b in range(3):
            source = jnp.concatenate([xcs[b, a], xcs[b, a + 1]], axis=1)
            out = dot(picked[b], source, NT)
            for d in range(BLOCKS[b]):
                block = 32 * a + FIRST[b] + d
                where = (block // 2) % NZL, block % 2
                rows = slice(block // NM * 8, block // NM * 8 + 8)
                for u in range(NX):
                    piece = out[d * 32 + u * 8 : d * 32 + u * 8 + 8]
                    if d == 0 and b > 0:
                        gacc[where[0], where[1], u, rows, :] += piece
                    else:
                        gacc[where[0], where[1], u, rows, :] = piece

    def send_core(k):
        return pltpu.make_async_remote_copy(
            src_ref=s1.at[k], dst_ref=r1.at[k], send_sem=c1s.at[k], recv_sem=c1r.at[k],
            device_id={"core": 1 - co}, device_id_type=pl.DeviceIdType.MESH,
        )

    pair = xx + 1 - 2 * (xx % 2)
    mirror = 3 - xx

    def partners(k):
        return (pair, mirror) if k < 3 else (mirror, pair)

    def second_of_first(k):
        first = partners(k)[0]
        return 3 - first if k < 3 else first + 1 - 2 * (first % 2)

    def send_x1(k):
        return pltpu.make_async_remote_copy(
            src_ref=s2.at[k], dst_ref=r2.at[k], send_sem=c2s.at[k], recv_sem=c2r.at[k],
            device_id={"x": partners(k)[0]}, device_id_type=pl.DeviceIdType.MESH,
        )

    def send_x2(k):
        return pltpu.make_async_remote_copy(
            src_ref=s3.at[k], dst_ref=r3.at[k], send_sem=c3s.at[k], recv_sem=c3r.at[k],
            device_id={"x": partners(k)[1]}, device_id_type=pl.DeviceIdType.MESH,
        )

    def y_copy(k, i, slot, src, t):
        return pltpu.make_async_remote_copy(
            src_ref=s4.at[k, src], dst_ref=r4.at[k, slot], send_sem=c4s.at[k, i],
            recv_sem=c4r.at[k, slot], device_id={"y": t}, device_id_type=pl.DeviceIdType.MESH,
        )

    def z_copy(k, h, slot):
        return pltpu.make_async_remote_copy(
            src_ref=s5.at[k], dst_ref=r5.at[slot], send_sem=c5s.at[k, h], recv_sem=c5r.at[slot],
            device_id={"zl": k, "zh": h}, device_id_type=pl.DeviceIdType.MESH,
        )

    def g_copy(i, slot, t):
        return pltpu.make_async_remote_copy(
            src_ref=r6.at[slot], dst_ref=r6.at[slot], send_sem=c6s.at[i], recv_sem=c6r.at[slot],
            device_id={"x": t}, device_id_type=pl.DeviceIdType.MESH,
        )

    def summed(k, u):
        return gacc[k, co, u] + r1[k, u].astype(f32)

    def step_x1(k):
        send_core(k).wait_recv()
        s2[k, 0] = summed(k, partners(k)[0]).astype(bf16)
        s2[k, 1] = summed(k, second_of_first(k)).astype(bf16)
        send_x1(k).start()

    def step_x2(k):
        send_x1(k).wait_recv()
        s3[k] = (summed(k, partners(k)[1]) + r2[k, 1].astype(f32)).astype(bf16)
        send_x2(k).start()

    def step_y(k):
        send_x2(k).wait_recv()
        val = (summed(k, xx) + r2[k, 0].astype(f32) + r3[k].astype(f32)).reshape(NY, 8, PAD)
        bown[k] = val
        s4[k] = val.astype(bf16)

        def go(i, c):
            t = (yy + i) % NY
            y_copy(k, i, yy, t, t).start()
            return c

        lax.fori_loop(1, NY, go, 0)

    def step_z(k):
        def go(i, acc):
            t = (yy + i) % NY
            y_copy(k, i, t, t, t).wait_recv()
            return acc + r4[k, t].astype(f32)

        val = lax.fori_loop(1, NY, go, bown[k, yy])
        cown[k] = val
        s5[k] = val.astype(bf16)
        for h in range(NZH):
            @pl.when(jnp.logical_or(zl != k, zh != h))
            def _():
                z_copy(k, h, z12).start()

    for k in ORDER:
        s1[k] = gacc[k, 1 - co].astype(bf16)
        send_core(k).start()

    row_n = jnp.sum(total2, axis=0, keepdims=True) / COUNT
    mean_n = column(row_n, 2)
    square_n = column(row_n, 3)
    rstd_n = lax.rsqrt(square_n - mean_n * mean_n + EPS)
    affine_n = (zn[...] - mean_n) * rstd_n * gam[...] + bet[...]
    y_next = (affine_n * jax.nn.sigmoid(affine_n)).astype(bf16)
    y_out[0, 0] = y_next[:, :COLS]
    y_out[0, 1] = y_next[:, COLS:]

    for k in ORDER:
        step_x1(k)

    @pl.when(has_prev)
    def _():
        gz_next.wait_recv()

    @pl.when(jnp.logical_not(has_prev))
    def _():
        gzh[0] = jnp.zeros((CH, COLS), bf16)

    @pl.when(has_next)
    def _():
        gz_prev.wait_recv()

    @pl.when(jnp.logical_not(has_next))
    def _():
        gzh[1] = jnp.zeros((CH, COLS), bf16)

    put_shifts(gzs, 0, gzh[0])
    put_shifts(gzs, 1, gzo[0])
    put_shifts(gzs, 2, gzo[1])
    put_shifts(gzs, 3, gzh[1])
    zc[...] = jnp.zeros_like(zc)

    def back(t, c):
        a, b = t // 3, t % 3
        source = jnp.concatenate([gzs[2 - b, 2 - a, :CH], gzs[2 - b, 3 - a, :CH]], axis=1)
        zc[...] += dot(kv[a, b], source, TN)
        return c

    lax.fori_loop(0, 9, back, 0)
    grad_x = zc[...].astype(bf16)
    gx_out[0, 0] = grad_x[:, :COLS]
    gx_out[0, 1] = grad_x[:, COLS:]

    for step in range(len(ORDER) + 5):
        if step < 6:
            step_x2(ORDER[step])
        if 2 <= step < 8:
            step_y(ORDER[step - 2])
        if 5 <= step < 11:
            step_z(ORDER[step - 5])

    def gather_z(i, acc):
        t = (z12 + i) % NZ
        z_copy(0, 0, t).wait_recv()
        return acc + r5[t].astype(f32)

    final = lax.fori_loop(1, NZ, gather_z, cown[zl])
    r6[xx] = final

    def go_x(i, c):
        g_copy(i, xx, (xx + i) % NX).start()
        return c

    lax.fori_loop(1, NX, go_x, 0)

    @pl.when(has_next)
    def _():
        halos[0].wait_send()
        halos[2].wait_send()
        gz_next.wait_send()

    @pl.when(has_prev)
    def _():
        halos[1].wait_send()
        halos[3].wait_send()
        gz_prev.wait_send()

    sent_all(a_copy, ra, as_, ar, m, NM)
    sent_all(b_copy, rb, bs, br, yy, NY)
    sent_all(a_copy, ra2, as2, ar2, m, NM)
    sent_all(b_copy, rb2, bs2, br2, yy, NY)
    for k in range(NZL):
        send_core(k).wait_send()
        send_x1(k).wait_send()
        send_x2(k).wait_send()

        def sent_y(i, c):
            y_copy(k, i, yy, (yy + i) % NY, (yy + i) % NY).wait_send()
            return c

        lax.fori_loop(1, NY, sent_y, 0)
        for h in range(NZH):
            @pl.when(jnp.logical_or(zl != k, zh != h))
            def _():
                z_copy(k, h, z12).wait_send()

    def end_x(i, c):
        t = (xx + i) % NX
        g_copy(i, t, t).wait_recv()
        g_copy(i, xx, t).wait_send()
        return c

    lax.fori_loop(1, NX, end_x, 0)
    gk_out[...] = r6[...]


def local(x_next, x_cur, grad_out, kernel, gamma, beta):
    any_spec = pl.BlockSpec(memory_space=pl.ANY)
    vmem = pl.BlockSpec(memory_space=pltpu.VMEM)
    dma = pltpu.SemaphoreType.DMA
    V = pltpu.VMEM
    scratch = [
        V((4, CH, COLS), bf16), V((4, CH, COLS), bf16), V((2, CH, COLS), bf16),
        V((3, 3, CH, CH), bf16),
        V((3, 4, PAD, COLS), bf16), V((3, 4, CH, COLS), bf16),
        V((2, CH, COLS), bf16), V((2, CH, COLS), bf16), V((3, 4, CH, COLS), bf16),
        V((CH, 2 * COLS), f32), V((CH, 2 * COLS), f32), V((CH, 2 * COLS), f32), V((CH, 2 * COLS), f32),
        V((CH, COLS), f32), V((CH, 1), f32), V((CH, 1), f32),
        V((3, 32 * max(BLOCKS), CH), bf16),
        V((NM, 8, COLS), f32), V((NY, 8, COLS), f32), V((NM, 8, COLS), f32), V((NY, 8, COLS), f32),
        V((NZL, NC, NX, NY * 8, PAD), f32),
        V((NZL, NX, NY * 8, PAD), bf16), V((NZL, NX, NY * 8, PAD), bf16),
        V((NZL, 2, NY * 8, PAD), bf16), V((NZL, 2, NY * 8, PAD), bf16),
        V((NZL, NY * 8, PAD), bf16), V((NZL, NY * 8, PAD), bf16),
        V((NZL, NY, 8, PAD), bf16), V((NZL, NY, 8, PAD), bf16),
        V((NZL, NY, 8, PAD), f32),
        V((NZL, 8, PAD), bf16), V((NZL, 8, PAD), f32),
        V((NZ, 8, PAD), bf16), V((NX, 8, PAD), f32),
        dma((4,)), dma((4,)), dma((4,)), dma((2,)), dma((2,)),
        dma((NM,)), dma((NM,)), dma((NY,)), dma((NY,)),
        dma((NM,)), dma((NM,)), dma((NY,)), dma((NY,)),
        dma((NZL,)), dma((NZL,)), dma((NZL,)), dma((NZL,)), dma((NZL,)), dma((NZL,)),
        dma((NZL, NY)), dma((NZL, NY)), dma((NZL, NZH)), dma((NZ,)), dma((NX,)), dma((NX,)),
    ]
    y_next, grad_x, quarters = pl.pallas_call(
        body,
        out_shape=(
            jax.ShapeDtypeStruct(x_next.shape, bf16),
            jax.ShapeDtypeStruct(x_next.shape, bf16),
            jax.ShapeDtypeStruct((NX, 8, PAD), f32),
        ),
        in_specs=[any_spec, any_spec, any_spec, any_spec, vmem, vmem],
        out_specs=(vmem, vmem, vmem),
        scratch_shapes=scratch,
        compiler_params=pltpu.CompilerParams(
            collective_id=0, has_side_effects=True, vmem_limit_bytes=60 * 1024 * 1024
        ),
    )(x_next, x_cur, grad_out, kernel, gamma.reshape(1, CH), beta.reshape(1, CH))
    half = lax.dynamic_slice_in_dim(
        quarters.reshape(NX, NZH, 4, PAD), lax.axis_index("zh"), 1, axis=1
    )
    flat = half[:, 0, :, :CH].reshape(-1)
    grad_kernel = lax.dynamic_slice_in_dim(flat, 1200 * lax.axis_index("x"), 1200)
    return y_next, grad_x, grad_kernel


def solution(mesh):
    torus = Mesh(mesh.devices.reshape(NY, NZL, NC, NZH, NX), HEIGHT + DP)
    image = P(DP, HEIGHT, None, None)
    return jax.shard_map(
        local,
        mesh=torus,
        in_specs=(image, image, image, P(), P(), P()),
        out_specs=(image, image, P(HEIGHT + DP)),
        check_vma=False,
    )
```

```python
import jax
import jax.numpy as jnp
from jax import lax
from jax.experimental import pallas as pl
from jax.experimental.pallas import tpu as pltpu
from jax.sharding import Mesh
from jax.sharding import PartitionSpec as P

CH = 320
COLS = 128
LANES = 128
MAIN = 256
REST = CH - MAIN
TALL = 160
GROUP = 10
NY, NZL, NC, NZH, NX = 8, 6, 2, 2, 4
NM = NZL * NC
NH = NY * NM
NZ = NZL * NZH
COUNT = 192 * GROUP * COLS
EPS = 1e-05
HEIGHT = ("y", "zl", "core")
DP = ("zh", "x")
FIRST = (0, 10, 21)
BLOCKS = (11, 12, 11)
ORDER = (0, 3, 1, 4, 2, 5)

f32 = jnp.float32
bf16 = jnp.bfloat16


def dot(a, b, dims=(((1,), (0,)), ((), ()))):
    return lax.dot_general(a, b, dims, preferred_element_type=f32)


NT = (((1,), (1,)), ((), ()))
TN = (((0,), (0,)), ((), ()))


def body(
    xn_in, xc_in, go_in, k_in, gam_in, bet_in,
    y_out, gx_out, gk_out,
    xcr, xnr, gor, kv, xcs, xhi, xns, gzo, gzh, gzs,
    zc, zn, nrm, gn, emask, gam, bet, selm,
    ra, rb, ra2, rb2,
    gacc, s1, r1, s2, r2, s3, r3, s4, r4, bown, s5, cown, r5, r6,
    lsem, hs, hr, ghs, ghr, as_, ar, bs, br, as2, ar2, bs2, br2,
    c1s, c1r, c2s, c2r, c3s, c3r, c4s, c4r, c5s, c5r, c6s, c6r,
):
    yy, zl, co = lax.axis_index("y"), lax.axis_index("zl"), lax.axis_index("core")
    zh, xx = lax.axis_index("zh"), lax.axis_index("x")
    m = zl * NC + co
    pos = yy * NM + m
    z12 = zl * NZH + zh

    def height_id(p):
        return {"y": p // NM, "zl": (p // NC) % NZL, "core": p % NC}

    has_prev, has_next = pos > 0, pos < NH - 1
    prev_id, next_id = height_id(jnp.maximum(pos - 1, 0)), height_id(jnp.minimum(pos + 1, NH - 1))

    barrier = pltpu.get_barrier_semaphore()

    def greet(device_id):
        pl.semaphore_signal(barrier, inc=1, device_id=device_id, device_id_type=pl.DeviceIdType.MESH)

    @pl.when(has_prev)
    def _():
        greet(prev_id)

    @pl.when(has_next)
    def _():
        greet(next_id)

    def far_z(i, c):
        greet({"zl": i, "zh": 1 - zh})
        return c

    lax.fori_loop(0, NZL, far_z, 0)

    def far_m(i, c):
        t = (m + i) % NM
        greet({"zl": t // NC, "core": t % NC})
        return c

    lax.fori_loop(1, NM, far_m, 0)

    def far_y(i, c):
        greet({"y": (yy + i) % NY})
        return c

    lax.fori_loop(1, NY, far_y, 0)

    def far_x(i, c):
        greet({"x": (xx + i) % NX})
        return c

    lax.fori_loop(1, NX, far_x, 0)

    cp_xc = pltpu.make_async_copy(xc_in.at[0], xcr.at[pl.ds(1, 2)], lsem.at[0])
    cp_k = pltpu.make_async_copy(k_in, kv, lsem.at[1])
    cp_xn = pltpu.make_async_copy(xn_in.at[0], xnr.at[pl.ds(1, 2)], lsem.at[2])
    cp_go = pltpu.make_async_copy(go_in.at[0], gor, lsem.at[3])
    for cp in (cp_xc, cp_k, cp_xn, cp_go):
        cp.start()

    rows_i = lax.broadcasted_iota(jnp.int32, (CH, COLS), 0)
    lane_i = lax.broadcasted_iota(jnp.int32, (CH, COLS), 1)
    rel = rows_i - GROUP * (lane_i & 31)
    emask[...] = jnp.where((rel >= 0) & (rel < GROUP), 1.0, 0.0).astype(f32)
    eye = lax.broadcasted_iota(jnp.int32, (CH, CH), 0) == lax.broadcasted_iota(jnp.int32, (CH, CH), 1)
    gam[...] = jnp.sum(jnp.where(eye, gam_in[...].reshape(1, CH), 0.0), axis=1, keepdims=True)
    bet[...] = jnp.sum(jnp.where(eye, bet_in[...].reshape(1, CH), 0.0), axis=1, keepdims=True)
    zc[...] = jnp.zeros_like(zc)
    zn[...] = jnp.zeros_like(zn)
    for b in range(3):
        for r in range(4):
            xcs[b, r, CH:, :] = jnp.zeros((REST, COLS), bf16)
            xhi[b, r, :REST, :] = jnp.zeros((REST, COLS), bf16)

    lane = lax.broadcasted_iota(jnp.int32, (CH, COLS), 1)

    def put_shifts(dst, row, v, high=None):
        wide = v.astype(f32)
        moved = (
            jnp.where(lane == 0, 0.0, pltpu.roll(wide, 1, 1)).astype(bf16),
            v,
            jnp.where(lane == COLS - 1, 0.0, pltpu.roll(wide, COLS - 1, 1)).astype(bf16),
        )
        for b in range(3):
            dst[b, row, :CH, :] = moved[b]
            if high is not None:
                high[b, row, REST:, :] = moved[b][MAIN:]

    cp_xc.wait()
    put_shifts(xcs, 1, xcr[1], xhi)
    put_shifts(xcs, 2, xcr[2], xhi)

    core27 = NZL + (NM - 1) + (NY - 1) + (NX - 1)
    pl.semaphore_wait(barrier, core27 + has_prev.astype(jnp.int32) + has_next.astype(jnp.int32))

    def halo(src, dst, to_next, i, send, recv):
        return pltpu.make_async_remote_copy(
            src_ref=src.at[0, 1] if to_next else src.at[0, 0],
            dst_ref=dst.at[0] if to_next else dst.at[3],
            send_sem=send.at[i],
            recv_sem=recv.at[i],
            device_id=next_id if to_next else prev_id,
            device_id_type=pl.DeviceIdType.MESH,
        )

    halos = (
        halo(xc_in, xcr, True, 0, hs, hr),
        halo(xc_in, xcr, False, 1, hs, hr),
        halo(xn_in, xnr, True, 2, hs, hr),
        halo(xn_in, xnr, False, 3, hs, hr),
    )

    @pl.when(has_next)
    def _():
        halos[0].start()

    @pl.when(has_prev)
    def _():
        halos[1].start()

    cp_k.wait()

    def conv_inner(acc, xs):
        def go(b, c):
            x1, x2 = xs[b, 1, :CH], xs[b, 2, :CH]
            acc[...] += dot(kv[1, b], jnp.concatenate([x1, x2], axis=1))
            acc[:, COLS:] += dot(kv[0, b], x1)
            acc[:, :COLS] += dot(kv[2, b], x2)
            return c

        lax.fori_loop(0, 3, go, 0)

    def conv_outer(acc, xs):
        def go(b, c):
            acc[:, :COLS] += dot(kv[0, b], xs[b, 0, :CH])
            acc[:, COLS:] += dot(kv[2, b], xs[b, 3, :CH])
            return c

        lax.fori_loop(0, 3, go, 0)

    conv_inner(zc, xcs)

    for b in range(3):
        n = BLOCKS[b] * 32
        rho = lax.broadcasted_iota(jnp.int32, (n, CH), 0)
        col = lax.broadcasted_iota(jnp.int32, (n, CH), 1)
        part = ((rho >> 3) & 3) * 4 + (rho & 3)
        src = 30 * (FIRST[b] + (rho >> 5)) + 15 * ((rho >> 2) & 1) + part - CH * b
        selm[b, :n, :] = jnp.where((part < 15) & (src == col), 1.0, 0.0).astype(bf16)

    def halo_wait(raw, up, down):
        @pl.when(has_prev)
        def _():
            up.wait_recv()

        @pl.when(jnp.logical_not(has_prev))
        def _():
            raw[0] = jnp.zeros((CH, COLS), bf16)

        @pl.when(has_next)
        def _():
            down.wait_recv()

        @pl.when(jnp.logical_not(has_next))
        def _():
            raw[3] = jnp.zeros((CH, COLS), bf16)

    halo_wait(xcr, halos[0], halos[1])

    @pl.when(has_next)
    def _():
        halos[2].start()

    @pl.when(has_prev)
    def _():
        halos[3].start()

    put_shifts(xcs, 0, xcr[0], xhi)
    put_shifts(xcs, 3, xcr[3], xhi)
    conv_outer(zc, xcs)

    def tile_of(cols4):
        q = lane >> 5
        picked = jnp.zeros((CH, COLS), f32)
        for i, v in enumerate(cols4):
            picked = jnp.where(q == i, v, picked)
        return jnp.sum(picked * emask[...], axis=0, keepdims=True)

    def a_copy(buf, send, recv, i, slot, t):
        return pltpu.make_async_remote_copy(
            src_ref=buf.at[slot],
            dst_ref=buf.at[slot],
            send_sem=send.at[i],
            recv_sem=recv.at[slot],
            device_id={"zl": t // NC, "core": t % NC},
            device_id_type=pl.DeviceIdType.MESH,
        )

    def b_copy(buf, send, recv, i, slot, t):
        return pltpu.make_async_remote_copy(
            src_ref=buf.at[slot],
            dst_ref=buf.at[slot],
            send_sem=send.at[i],
            recv_sem=recv.at[slot],
            device_id={"y": t},
            device_id_type=pl.DeviceIdType.MESH,
        )

    def start_all(copy, buf, send, recv, me, n, tile):
        buf[me] = tile

        def go(i, c):
            copy(buf, send, recv, i, me, (me + i) % n).start()
            return c

        lax.fori_loop(1, n, go, 0)

    def wait_all(copy, buf, send, recv, me, n):
        def go(i, c):
            t = (me + i) % n
            copy(buf, send, recv, i, t, t).wait_recv()
            return c

        lax.fori_loop(1, n, go, 0)
        return jnp.sum(buf[...], axis=0)

    def sent_all(copy, buf, send, recv, me, n):
        def go(i, c):
            copy(buf, send, recv, i, me, (me + i) % n).wait_send()
            return c

        lax.fori_loop(1, n, go, 0)

    z = zc[...]
    start_all(
        a_copy, ra, as_, ar, m, NM,
        tile_of((jnp.sum(z, axis=1, keepdims=True), jnp.sum(z * z, axis=1, keepdims=True))),
    )

    cp_xn.wait()
    put_shifts(xns, 1, xnr[1])
    put_shifts(xns, 2, xnr[2])
    conv_inner(zn, xns)
    start_all(b_copy, rb, bs, br, yy, NY, wait_all(a_copy, ra, as_, ar, m, NM))
    halo_wait(xnr, halos[2], halos[3])
    put_shifts(xns, 0, xnr[0])
    put_shifts(xns, 3, xnr[3])
    conv_outer(zn, xns)
    zv = zn[...]
    next_sums = (jnp.sum(zv, axis=1, keepdims=True), jnp.sum(zv * zv, axis=1, keepdims=True))
    cp_go.wait()
    total = wait_all(b_copy, rb, bs, br, yy, NY)

    def column(row, block):
        keep = (lane >> 5) == block
        return jnp.sum(jnp.where(keep, emask[...] * row, 0.0), axis=1, keepdims=True)

    def moments(tile, first):
        row = tile / COUNT
        mean_row = pltpu.roll(jnp.broadcast_to(row, (8, COLS)), (128 - 32 * first) % 128, 1)[:1]
        square_row = pltpu.roll(jnp.broadcast_to(row, (8, COLS)), (128 - 32 * (first + 1)) % 128, 1)[:1]
        rstd_row = lax.rsqrt(square_row - mean_row * mean_row + EPS)
        return column(mean_row, 0), column(rstd_row, 0)

    mean_c, rstd_c = moments(total, 0)
    normed = (zc[...] - mean_c) * rstd_c
    nrm[...] = normed
    affine = normed * gam[...] + bet[...]
    sig = jax.nn.sigmoid(affine)
    grad = jnp.concatenate([gor[0], gor[1]], axis=1).astype(f32)
    grad_n = grad * (sig * (1.0 + affine * (1.0 - sig))) * gam[...]
    gn[...] = grad_n
    start_all(
        a_copy, ra2, as2, ar2, m, NM,
        tile_of(
            (
                jnp.sum(grad_n, axis=1, keepdims=True),
                jnp.sum(grad_n * normed, axis=1, keepdims=True),
            )
            + next_sums
        ),
    )
    start_all(b_copy, rb2, bs2, br2, yy, NY, wait_all(a_copy, ra2, as2, ar2, m, NM))
    total2 = wait_all(b_copy, rb2, bs2, br2, yy, NY)
    row2 = total2 / COUNT
    mean_1, mean_2 = column(row2, 0), column(row2, 1)
    gz = (rstd_c * (gn[...] - mean_1 - nrm[...] * mean_2)).astype(bf16)
    gzo[0] = gz[:, :COLS]
    gzo[1] = gz[:, COLS:]

    def gz_copy(to_next):
        return pltpu.make_async_remote_copy(
            src_ref=gzo.at[1] if to_next else gzo.at[0],
            dst_ref=gzh.at[0] if to_next else gzh.at[1],
            send_sem=ghs.at[0 if to_next else 1],
            recv_sem=ghr.at[0 if to_next else 1],
            device_id=next_id if to_next else prev_id,
            device_id_type=pl.DeviceIdType.MESH,
        )

    gz_next, gz_prev = gz_copy(True), gz_copy(False)

    @pl.when(has_next)
    def _():
        gz_next.start()

    @pl.when(has_prev)
    def _():
        gz_prev.start()

    picked = [dot(selm[b, : BLOCKS[b] * 32], gz).astype(bf16) for b in range(3)]

    def put(ref, rows, piece, add):
        if add:
            ref[rows, :] += piece
        else:
            ref[rows, :] = piece

    for a in range(3):
        for b in range(3):
            first = 32 * a + FIRST[b]
            low = min(max(NH // 2 - first, 0), BLOCKS[b])
            out = dot(picked[b], jnp.concatenate([xcs[b, a, :MAIN], xcs[b, a + 1, :MAIN]], axis=1), NT)
            rest = []
            if low > 0:
                source = jnp.concatenate([xcs[b, a, MAIN:], xcs[b, a + 1, MAIN:]], axis=1)
                rest.append(dot(picked[b][: low * 32], source, NT))
            if low < BLOCKS[b]:
                source = jnp.concatenate([xhi[b, a], xhi[b, a + 1]], axis=1)
                rest.append(dot(picked[b][low * 32 :], source, NT))
            for d in range(BLOCKS[b]):
                block = first + d
                row = block // NM
                part, at = (rest[0], d) if d < low else (rest[-1], d - low)
                again = d == 0 and b > 0
                for u in range(NX):
                    ref = gacc.at[(block // 2) % NZL, block % 2, u]
                    top = d * 32 + u * 8
                    put(ref, slice(row * 8, row * 8 + 8), out[top : top + 8, :LANES], again)
                    put(ref, slice(64 + row * 8, 72 + row * 8), out[top : top + 8, LANES:], again)
                    top = at * 32 + u * 8
                    at_row = 128 + row % 4 * 8
                    put(ref, slice(at_row, at_row + 8), part[top : top + 8], again or row >= 4)

    def send_core(k):
        return pltpu.make_async_remote_copy(
            src_ref=s1.at[k], dst_ref=r1.at[k], send_sem=c1s.at[k], recv_sem=c1r.at[k],
            device_id={"core": 1 - co}, device_id_type=pl.DeviceIdType.MESH,
        )

    pair = xx + 1 - 2 * (xx % 2)
    mirror = 3 - xx

    def partners(k):
        return (pair, mirror) if k < 3 else (mirror, pair)

    def second_of_first(k):
        first = partners(k)[0]
        return 3 - first if k < 3 else first + 1 - 2 * (first % 2)

    def send_x1(k):
        return pltpu.make_async_remote_copy(
            src_ref=s2.at[k], dst_ref=r2.at[k], send_sem=c2s.at[k], recv_sem=c2r.at[k],
            device_id={"x": partners(k)[0]}, device_id_type=pl.DeviceIdType.MESH,
        )

    def send_x2(k):
        return pltpu.make_async_remote_copy(
            src_ref=s3.at[k], dst_ref=r3.at[k], send_sem=c3s.at[k], recv_sem=c3r.at[k],
            device_id={"x": partners(k)[1]}, device_id_type=pl.DeviceIdType.MESH,
        )

    def y_copy(k, i, slot, src, t):
        return pltpu.make_async_remote_copy(
            src_ref=s4.at[k, src], dst_ref=r4.at[k, slot], send_sem=c4s.at[k, i],
            recv_sem=c4r.at[k, slot], device_id={"y": t}, device_id_type=pl.DeviceIdType.MESH,
        )

    def z_copy(k, h, slot):
        return pltpu.make_async_remote_copy(
            src_ref=s5.at[k], dst_ref=r5.at[slot], send_sem=c5s.at[k, h], recv_sem=c5r.at[slot],
            device_id={"zl": k, "zh": h}, device_id_type=pl.DeviceIdType.MESH,
        )

    def g_copy(i, slot, t):
        return pltpu.make_async_remote_copy(
            src_ref=r6.at[slot], dst_ref=r6.at[slot], send_sem=c6s.at[i], recv_sem=c6r.at[slot],
            device_id={"x": t}, device_id_type=pl.DeviceIdType.MESH,
        )

    def summed(k, u):
        return gacc[k, co, u] + r1[k, u].astype(f32)

    def step_x1(k):
        send_core(k).wait_recv()
        s2[k, 0] = summed(k, partners(k)[0]).astype(bf16)
        s2[k, 1] = summed(k, second_of_first(k)).astype(bf16)
        send_x1(k).start()

    def step_x2(k):
        send_x1(k).wait_recv()
        s3[k] = (summed(k, partners(k)[1]) + r2[k, 1].astype(f32)).astype(bf16)
        send_x2(k).start()

    def step_y(k):
        send_x2(k).wait_recv()
        val = summed(k, xx) + r2[k, 0].astype(f32) + r3[k].astype(f32)
        for i in range(2):
            bown[k, :, i * 8 : i * 8 + 8, :] = val[i * 64 : i * 64 + 64].reshape(NY, 8, LANES)
        rest = val[128:].reshape(NY // 2, 8, LANES)
        bown[k, : NY // 2, 16:, :] = rest
        bown[k, NY // 2 :, 16:, :] = rest
        s4[k] = bown[k].astype(bf16)

        def go(i, c):
            t = (yy + i) % NY
            y_copy(k, i, yy, t, t).start()
            return c

        lax.fori_loop(1, NY, go, 0)

    def step_z(k):
        def go(i, acc):
            t = (yy + i) % NY
            y_copy(k, i, t, t, t).wait_recv()
            return acc + r4[k, t].astype(f32)

        val = lax.fori_loop(1, NY, go, bown[k, yy])
        cown[k] = val
        s5[k] = val.astype(bf16)
        for h in range(NZH):
            @pl.when(jnp.logical_or(zl != k, zh != h))
            def _():
                z_copy(k, h, z12).start()

    for k in ORDER:
        s1[k] = gacc[k, 1 - co].astype(bf16)
        send_core(k).start()

    mean_n = column(row2, 2)
    square_n = column(row2, 3)
    rstd_n = lax.rsqrt(square_n - mean_n * mean_n + EPS)
    affine_n = (zn[...] - mean_n) * rstd_n * gam[...] + bet[...]
    y_next = (affine_n * jax.nn.sigmoid(affine_n)).astype(bf16)
    y_out[0, 0] = y_next[:, :COLS]
    y_out[0, 1] = y_next[:, COLS:]

    for k in ORDER:
        step_x1(k)

    @pl.when(has_prev)
    def _():
        gz_next.wait_recv()

    @pl.when(jnp.logical_not(has_prev))
    def _():
        gzh[0] = jnp.zeros((CH, COLS), bf16)

    @pl.when(has_next)
    def _():
        gz_prev.wait_recv()

    @pl.when(jnp.logical_not(has_next))
    def _():
        gzh[1] = jnp.zeros((CH, COLS), bf16)

    put_shifts(gzs, 0, gzh[0])
    put_shifts(gzs, 1, gzo[0])
    put_shifts(gzs, 2, gzo[1])
    put_shifts(gzs, 3, gzh[1])
    zc[...] = jnp.zeros_like(zc)

    def back(t, c):
        a, b = t // 3, t % 3
        source = jnp.concatenate([gzs[2 - b, 2 - a, :CH], gzs[2 - b, 3 - a, :CH]], axis=1)
        zc[...] += dot(kv[a, b], source, TN)
        return c

    lax.fori_loop(0, 9, back, 0)
    grad_x = zc[...].astype(bf16)
    gx_out[0, 0] = grad_x[:, :COLS]
    gx_out[0, 1] = grad_x[:, COLS:]

    for step in range(len(ORDER) + 5):
        if step < 6:
            step_x2(ORDER[step])
        if 2 <= step < 8:
            step_y(ORDER[step - 2])
        if 5 <= step < 11:
            step_z(ORDER[step - 5])

    def gather_z(i, acc):
        t = (z12 + i) % NZ
        z_copy(0, 0, t).wait_recv()
        return acc + r5[t].astype(f32)

    final = lax.fori_loop(1, NZ, gather_z, cown[zl])
    r6[xx] = final

    def go_x(i, c):
        g_copy(i, xx, (xx + i) % NX).start()
        return c

    lax.fori_loop(1, NX, go_x, 0)

    @pl.when(has_next)
    def _():
        halos[0].wait_send()
        halos[2].wait_send()
        gz_next.wait_send()

    @pl.when(has_prev)
    def _():
        halos[1].wait_send()
        halos[3].wait_send()
        gz_prev.wait_send()

    sent_all(a_copy, ra, as_, ar, m, NM)
    sent_all(b_copy, rb, bs, br, yy, NY)
    sent_all(a_copy, ra2, as2, ar2, m, NM)
    sent_all(b_copy, rb2, bs2, br2, yy, NY)
    for k in range(NZL):
        send_core(k).wait_send()
        send_x1(k).wait_send()
        send_x2(k).wait_send()

        def sent_y(i, c):
            y_copy(k, i, yy, (yy + i) % NY, (yy + i) % NY).wait_send()
            return c

        lax.fori_loop(1, NY, sent_y, 0)
        for h in range(NZH):
            @pl.when(jnp.logical_or(zl != k, zh != h))
            def _():
                z_copy(k, h, z12).wait_send()

    def end_x(i, c):
        t = (xx + i) % NX
        g_copy(i, t, t).wait_recv()
        g_copy(i, xx, t).wait_send()
        return c

    lax.fori_loop(1, NX, end_x, 0)
    gk_out[...] = r6[...]


def last(y_in, gx_in, raw, y_out, gx_out, gk_out, ybuf, gbuf, rows, sem):
    pairs = ((y_in, ybuf, y_out), (gx_in, gbuf, gx_out))
    into = [pltpu.make_async_copy(a, b, sem.at[i]) for i, (a, b, _) in enumerate(pairs)]
    back = [pltpu.make_async_copy(b, c, sem.at[2 + i]) for i, (_, b, c) in enumerate(pairs)]
    for cp in into:
        cp.start()
    second, high = lax.axis_index("zh") == 1, lax.axis_index("y") >= NY // 2
    for u in range(NX):
        tile = raw[u]
        rest = tile[16:]
        parts = (tile[:8], tile[8:16], jnp.where(high, pltpu.roll(rest, REST, 1), rest))
        for i, p in enumerate(parts):
            rows[u * 4 : u * 4 + 4, i * LANES : (i + 1) * LANES] = jnp.where(second, p[4:], p[:4])
    into[0].wait()
    back[0].start()
    into[1].wait()
    back[1].start()
    share = 9 * CH * CH // (NH * NZH * NX)
    for v in range(NX):

        @pl.when(lax.axis_index("x") == v)
        def _():
            for start in range(0, share, LANES):
                n = min(LANES, share - start)
                r, col = divmod(share * v + start, CH)
                k = min(n, CH - col)
                piece = rows[r : r + 1, col : col + k]
                if k < n:
                    piece = jnp.concatenate([piece, rows[r + 1 : r + 2, : n - k]], axis=1)
                gk_out[pl.ds(start, n)] = piece.reshape(n)

    for cp in back:
        cp.wait()


def local(x_next, x_cur, grad_out, kernel, gamma, beta):
    any_spec = pl.BlockSpec(memory_space=pl.ANY)
    vmem = pl.BlockSpec(memory_space=pltpu.VMEM)
    dma = pltpu.SemaphoreType.DMA
    V = pltpu.VMEM
    scratch = [
        V((4, CH, COLS), bf16), V((4, CH, COLS), bf16), V((2, CH, COLS), bf16),
        V((3, 3, CH, CH), bf16),
        V((3, 4, CH + REST, COLS), bf16), V((3, 4, 2 * REST, COLS), bf16), V((3, 4, CH, COLS), bf16),
        V((2, CH, COLS), bf16), V((2, CH, COLS), bf16), V((3, 4, CH, COLS), bf16),
        V((CH, 2 * COLS), f32), V((CH, 2 * COLS), f32), V((CH, 2 * COLS), f32), V((CH, 2 * COLS), f32),
        V((CH, COLS), f32), V((CH, 1), f32), V((CH, 1), f32),
        V((3, 32 * max(BLOCKS), CH), bf16),
        V((NM, 1, COLS), f32), V((NY, 1, COLS), f32), V((NM, 1, COLS), f32), V((NY, 1, COLS), f32),
        V((NZL, NC, NX, TALL, LANES), f32),
        V((NZL, NX, TALL, LANES), bf16), V((NZL, NX, TALL, LANES), bf16),
        V((NZL, 2, TALL, LANES), bf16), V((NZL, 2, TALL, LANES), bf16),
        V((NZL, TALL, LANES), bf16), V((NZL, TALL, LANES), bf16),
        V((NZL, NY, 24, LANES), bf16), V((NZL, NY, 24, LANES), bf16),
        V((NZL, NY, 24, LANES), f32),
        V((NZL, 24, LANES), bf16), V((NZL, 24, LANES), f32),
        V((NZ, 24, LANES), bf16), V((NX, 24, LANES), f32),
        dma((4,)), dma((4,)), dma((4,)), dma((2,)), dma((2,)),
        dma((NM,)), dma((NM,)), dma((NY,)), dma((NY,)),
        dma((NM,)), dma((NM,)), dma((NY,)), dma((NY,)),
        dma((NZL,)), dma((NZL,)), dma((NZL,)), dma((NZL,)), dma((NZL,)), dma((NZL,)),
        dma((NZL, NY)), dma((NZL, NY)), dma((NZL, NZH)), dma((NZ,)), dma((NX,)), dma((NX,)),
    ]
    y_next, grad_x, quarters = pl.pallas_call(
        body,
        out_shape=(
            jax.ShapeDtypeStruct(x_next.shape, bf16),
            jax.ShapeDtypeStruct(x_next.shape, bf16),
            jax.ShapeDtypeStruct((NX, 24, LANES), f32),
        ),
        in_specs=[any_spec, any_spec, any_spec, any_spec, vmem, vmem],
        out_specs=(vmem, vmem, vmem),
        scratch_shapes=scratch,
        compiler_params=pltpu.CompilerParams(
            collective_id=0, has_side_effects=True, vmem_limit_bytes=60 * 1024 * 1024
        ),
    )(x_next, x_cur, grad_out, kernel, gamma, beta)
    return pl.pallas_call(
        last,
        out_shape=(
            jax.ShapeDtypeStruct(x_next.shape, bf16),
            jax.ShapeDtypeStruct(x_next.shape, bf16),
            jax.ShapeDtypeStruct((9 * CH * CH // (NH * NZH * NX),), f32),
        ),
        in_specs=[any_spec, any_spec, vmem],
        out_specs=(any_spec, any_spec, vmem),
        scratch_shapes=[V(x_next.shape, bf16), V(x_next.shape, bf16), V((16, 3 * LANES), f32), dma((4,))],
    )(y_next, grad_x, quarters)


def solution(mesh):
    torus = Mesh(mesh.devices.reshape(NY, NZL, NC, NZH, NX), HEIGHT + DP)
    image = P(DP, HEIGHT, None, None)
    return jax.shard_map(
        local,
        mesh=torus,
        in_specs=(image, image, image, P(), P(), P()),
        out_specs=(image, image, P(HEIGHT + DP)),
        check_vma=False,
    )
```

```python
import jax
import jax.numpy as jnp
from jax import lax
from jax.experimental import pallas as pl
from jax.experimental.pallas import tpu as pltpu
from jax.sharding import Mesh
from jax.sharding import PartitionSpec as P

CH = 320
COLS = 128
LANES = 128
MAIN = 256
REST = CH - MAIN
TALL = 160
GROUP = 10
NY, NZL, NC, NZH, NX = 8, 6, 2, 2, 4
NM = NZL * NC
NH = NY * NM
NZ = NZL * NZH
COUNT = 192 * GROUP * COLS
EPS = 1e-05
HEIGHT = ("y", "zl", "core")
DP = ("zh", "x")
FIRST = (0, 10, 21)
BLOCKS = (11, 12, 11)
ORDER = (0, 3, 1, 4, 2, 5)

f32 = jnp.float32
bf16 = jnp.bfloat16


def dot(a, b, dims=(((1,), (0,)), ((), ()))):
    return lax.dot_general(a, b, dims, preferred_element_type=f32)


NT = (((1,), (1,)), ((), ()))
TN = (((0,), (0,)), ((), ()))


def body(
    xn_in, xc_in, go_in, k_in, gam_in, bet_in,
    y_out, gx_out, gk_out,
    gam_row, bet_row, xcr, xnr, gor, kv, xcs, xhi, xns, gzo, gzh, gzs,
    zc, zn, nrm, gn, emask, gam, bet, selm,
    ra, rb, ra2, rb2,
    gacc, s1, r1, s2, r2, s3, r3, s4, r4, bown, s5, cown, r5, mine, before,
    lsem, hs, hr, ghs, ghr, as_, ar, bs, br, as2, ar2, bs2, br2,
    c1s, c1r, c2s, c2r, c3s, c3r, c4s, c4r, c5s, c5r, fsem,
):
    yy, zl, co = lax.axis_index("y"), lax.axis_index("zl"), lax.axis_index("core")
    zh, xx = lax.axis_index("zh"), lax.axis_index("x")
    m = zl * NC + co
    pos = yy * NM + m
    z12 = zl * NZH + zh

    def height_id(p):
        return {"y": p // NM, "zl": (p // NC) % NZL, "core": p % NC}

    has_prev, has_next = pos > 0, pos < NH - 1
    prev_id, next_id = height_id(jnp.maximum(pos - 1, 0)), height_id(jnp.minimum(pos + 1, NH - 1))

    barrier = pltpu.get_barrier_semaphore()

    def greet(device_id):
        pl.semaphore_signal(barrier, inc=1, device_id=device_id, device_id_type=pl.DeviceIdType.MESH)

    @pl.when(has_prev)
    def _():
        greet(prev_id)

    @pl.when(has_next)
    def _():
        greet(next_id)

    def far_z(i, c):
        greet({"zl": i, "zh": 1 - zh})
        return c

    lax.fori_loop(0, NZL, far_z, 0)

    def far_m(i, c):
        t = (m + i) % NM
        greet({"zl": t // NC, "core": t % NC})
        return c

    lax.fori_loop(1, NM, far_m, 0)

    def far_y(i, c):
        greet({"y": (yy + i) % NY})
        return c

    lax.fori_loop(1, NY, far_y, 0)

    def far_x(i, c):
        greet({"x": (xx + i) % NX})
        return c

    lax.fori_loop(1, NX, far_x, 0)

    cp_xc = pltpu.make_async_copy(xc_in.at[0], xcr.at[pl.ds(1, 2)], lsem.at[0])
    cp_k = pltpu.make_async_copy(k_in, kv, lsem.at[1])
    cp_xn = pltpu.make_async_copy(xn_in.at[0], xnr.at[pl.ds(1, 2)], lsem.at[2])
    cp_go = pltpu.make_async_copy(go_in.at[0], gor, lsem.at[3])
    cp_gam = pltpu.make_async_copy(gam_in, gam_row, lsem.at[4])
    cp_bet = pltpu.make_async_copy(bet_in, bet_row, lsem.at[5])
    for cp in (cp_xc, cp_gam, cp_bet, cp_k, cp_xn, cp_go):
        cp.start()

    greeted = NZL + (NM - 1) + (NY - 1) + (NX - 1)
    pl.semaphore_wait(barrier, greeted + has_prev.astype(jnp.int32) + has_next.astype(jnp.int32))

    def halo(src, dst, to_next, i, send, recv):
        return pltpu.make_async_remote_copy(
            src_ref=src.at[0, 1] if to_next else src.at[0, 0],
            dst_ref=dst.at[0] if to_next else dst.at[3],
            send_sem=send.at[i],
            recv_sem=recv.at[i],
            device_id=next_id if to_next else prev_id,
            device_id_type=pl.DeviceIdType.MESH,
        )

    halos = (
        halo(xc_in, xcr, True, 0, hs, hr),
        halo(xc_in, xcr, False, 1, hs, hr),
        halo(xn_in, xnr, True, 2, hs, hr),
        halo(xn_in, xnr, False, 3, hs, hr),
    )

    @pl.when(has_next)
    def _():
        halos[0].start()

    @pl.when(has_prev)
    def _():
        halos[1].start()

    rows_i = lax.broadcasted_iota(jnp.int32, (CH, COLS), 0)
    lane_i = lax.broadcasted_iota(jnp.int32, (CH, COLS), 1)
    rel = rows_i - GROUP * (lane_i & 31)
    emask[...] = jnp.where((rel >= 0) & (rel < GROUP), 1.0, 0.0).astype(f32)
    eye = lax.broadcasted_iota(jnp.int32, (CH, CH), 0) == lax.broadcasted_iota(jnp.int32, (CH, CH), 1)
    cp_gam.wait()
    cp_bet.wait()
    gam[...] = jnp.sum(jnp.where(eye, gam_row[...].reshape(1, CH), 0.0), axis=1, keepdims=True)
    bet[...] = jnp.sum(jnp.where(eye, bet_row[...].reshape(1, CH), 0.0), axis=1, keepdims=True)
    zc[...] = jnp.zeros_like(zc)
    zn[...] = jnp.zeros_like(zn)
    for b in range(3):
        for r in range(4):
            xcs[b, r, CH:, :] = jnp.zeros((REST, COLS), bf16)
            xhi[b, r, :REST, :] = jnp.zeros((REST, COLS), bf16)

    lane = lax.broadcasted_iota(jnp.int32, (CH, COLS), 1)

    def put_shifts(dst, row, v, high=None):
        wide = v.astype(f32)
        moved = (
            jnp.where(lane == 0, 0.0, pltpu.roll(wide, 1, 1)).astype(bf16),
            v,
            jnp.where(lane == COLS - 1, 0.0, pltpu.roll(wide, COLS - 1, 1)).astype(bf16),
        )
        for b in range(3):
            dst[b, row, :CH, :] = moved[b]
            if high is not None:
                high[b, row, REST:, :] = moved[b][MAIN:]

    cp_xc.wait()
    put_shifts(xcs, 1, xcr[1], xhi)
    put_shifts(xcs, 2, xcr[2], xhi)

    cp_k.wait()

    def conv_inner(acc, xs):
        def go(b, c):
            x1, x2 = xs[b, 1, :CH], xs[b, 2, :CH]
            acc[...] += dot(kv[1, b], jnp.concatenate([x1, x2], axis=1))
            acc[:, COLS:] += dot(kv[0, b], x1)
            acc[:, :COLS] += dot(kv[2, b], x2)
            return c

        lax.fori_loop(0, 3, go, 0)

    def conv_outer(acc, xs):
        def go(b, c):
            acc[:, :COLS] += dot(kv[0, b], xs[b, 0, :CH])
            acc[:, COLS:] += dot(kv[2, b], xs[b, 3, :CH])
            return c

        lax.fori_loop(0, 3, go, 0)

    conv_inner(zc, xcs)

    for b in range(3):
        n = BLOCKS[b] * 32
        rho = lax.broadcasted_iota(jnp.int32, (n, CH), 0)
        col = lax.broadcasted_iota(jnp.int32, (n, CH), 1)
        part = ((rho >> 3) & 3) * 4 + (rho & 3)
        src = 30 * (FIRST[b] + (rho >> 5)) + 15 * ((rho >> 2) & 1) + part - CH * b
        selm[b, :n, :] = jnp.where((part < 15) & (src == col), 1.0, 0.0).astype(bf16)

    def halo_wait(raw, up, down):
        @pl.when(has_prev)
        def _():
            up.wait_recv()

        @pl.when(jnp.logical_not(has_prev))
        def _():
            raw[0] = jnp.zeros((CH, COLS), bf16)

        @pl.when(has_next)
        def _():
            down.wait_recv()

        @pl.when(jnp.logical_not(has_next))
        def _():
            raw[3] = jnp.zeros((CH, COLS), bf16)

    halo_wait(xcr, halos[0], halos[1])

    @pl.when(has_next)
    def _():
        halos[2].start()

    @pl.when(has_prev)
    def _():
        halos[3].start()

    put_shifts(xcs, 0, xcr[0], xhi)
    put_shifts(xcs, 3, xcr[3], xhi)
    conv_outer(zc, xcs)

    def tile_of(cols4):
        q = lane >> 5
        picked = jnp.zeros((CH, COLS), f32)
        for i, v in enumerate(cols4):
            picked = jnp.where(q == i, v, picked)
        return jnp.sum(picked * emask[...], axis=0, keepdims=True)

    def a_copy(buf, send, recv, i, slot, t):
        return pltpu.make_async_remote_copy(
            src_ref=buf.at[slot],
            dst_ref=buf.at[slot],
            send_sem=send.at[i],
            recv_sem=recv.at[slot],
            device_id={"zl": t // NC, "core": t % NC},
            device_id_type=pl.DeviceIdType.MESH,
        )

    def b_copy(buf, send, recv, i, slot, t):
        return pltpu.make_async_remote_copy(
            src_ref=buf.at[slot],
            dst_ref=buf.at[slot],
            send_sem=send.at[i],
            recv_sem=recv.at[slot],
            device_id={"y": t},
            device_id_type=pl.DeviceIdType.MESH,
        )

    def start_all(copy, buf, send, recv, me, n, tile):
        buf[me] = tile

        def go(i, c):
            copy(buf, send, recv, i, me, (me + i) % n).start()
            return c

        lax.fori_loop(1, n, go, 0)

    def wait_all(copy, buf, send, recv, me, n):
        def go(i, c):
            t = (me + i) % n
            copy(buf, send, recv, i, t, t).wait_recv()
            return c

        lax.fori_loop(1, n, go, 0)
        return jnp.sum(buf[...], axis=0)

    def sent_all(copy, buf, send, recv, me, n):
        def go(i, c):
            copy(buf, send, recv, i, me, (me + i) % n).wait_send()
            return c

        lax.fori_loop(1, n, go, 0)

    z = zc[...]
    start_all(
        a_copy, ra, as_, ar, m, NM,
        tile_of((jnp.sum(z, axis=1, keepdims=True), jnp.sum(z * z, axis=1, keepdims=True))),
    )

    cp_xn.wait()
    put_shifts(xns, 1, xnr[1])
    put_shifts(xns, 2, xnr[2])
    conv_inner(zn, xns)
    start_all(b_copy, rb, bs, br, yy, NY, wait_all(a_copy, ra, as_, ar, m, NM))
    halo_wait(xnr, halos[2], halos[3])
    put_shifts(xns, 0, xnr[0])
    put_shifts(xns, 3, xnr[3])
    conv_outer(zn, xns)
    zv = zn[...]
    next_sums = (jnp.sum(zv, axis=1, keepdims=True), jnp.sum(zv * zv, axis=1, keepdims=True))
    cp_go.wait()
    total = wait_all(b_copy, rb, bs, br, yy, NY)

    def column(row, block):
        keep = (lane >> 5) == block
        return jnp.sum(jnp.where(keep, emask[...] * row, 0.0), axis=1, keepdims=True)

    def moments(tile, first):
        row = tile / COUNT
        mean_row = pltpu.roll(jnp.broadcast_to(row, (8, COLS)), (128 - 32 * first) % 128, 1)[:1]
        square_row = pltpu.roll(jnp.broadcast_to(row, (8, COLS)), (128 - 32 * (first + 1)) % 128, 1)[:1]
        rstd_row = lax.rsqrt(square_row - mean_row * mean_row + EPS)
        return column(mean_row, 0), column(rstd_row, 0)

    mean_c, rstd_c = moments(total, 0)
    normed = (zc[...] - mean_c) * rstd_c
    nrm[...] = normed
    affine = normed * gam[...] + bet[...]
    sig = jax.nn.sigmoid(affine)
    grad = jnp.concatenate([gor[0], gor[1]], axis=1).astype(f32)
    grad_n = grad * (sig * (1.0 + affine * (1.0 - sig))) * gam[...]
    gn[...] = grad_n
    start_all(
        a_copy, ra2, as2, ar2, m, NM,
        tile_of(
            (
                jnp.sum(grad_n, axis=1, keepdims=True),
                jnp.sum(grad_n * normed, axis=1, keepdims=True),
            )
            + next_sums
        ),
    )
    start_all(b_copy, rb2, bs2, br2, yy, NY, wait_all(a_copy, ra2, as2, ar2, m, NM))
    total2 = wait_all(b_copy, rb2, bs2, br2, yy, NY)
    row2 = total2 / COUNT
    mean_1, mean_2 = column(row2, 0), column(row2, 1)
    gz = (rstd_c * (gn[...] - mean_1 - nrm[...] * mean_2)).astype(bf16)
    gzo[0] = gz[:, :COLS]
    gzo[1] = gz[:, COLS:]

    def gz_copy(to_next):
        return pltpu.make_async_remote_copy(
            src_ref=gzo.at[1] if to_next else gzo.at[0],
            dst_ref=gzh.at[0] if to_next else gzh.at[1],
            send_sem=ghs.at[0 if to_next else 1],
            recv_sem=ghr.at[0 if to_next else 1],
            device_id=next_id if to_next else prev_id,
            device_id_type=pl.DeviceIdType.MESH,
        )

    gz_next, gz_prev = gz_copy(True), gz_copy(False)

    @pl.when(has_next)
    def _():
        gz_next.start()

    @pl.when(has_prev)
    def _():
        gz_prev.start()

    picked = [dot(selm[b, : BLOCKS[b] * 32], gz).astype(bf16) for b in range(3)]

    def put(ref, rows, piece, add):
        if add:
            ref[rows, :] += piece
        else:
            ref[rows, :] = piece

    for a in range(3):
        for b in range(3):
            first = 32 * a + FIRST[b]
            low = min(max(NH // 2 - first, 0), BLOCKS[b])
            out = dot(picked[b], jnp.concatenate([xcs[b, a, :MAIN], xcs[b, a + 1, :MAIN]], axis=1), NT)
            rest = []
            if low > 0:
                source = jnp.concatenate([xcs[b, a, MAIN:], xcs[b, a + 1, MAIN:]], axis=1)
                rest.append(dot(picked[b][: low * 32], source, NT))
            if low < BLOCKS[b]:
                source = jnp.concatenate([xhi[b, a], xhi[b, a + 1]], axis=1)
                rest.append(dot(picked[b][low * 32 :], source, NT))
            for d in range(BLOCKS[b]):
                block = first + d
                row = block // NM
                part, at = (rest[0], d) if d < low else (rest[-1], d - low)
                again = d == 0 and b > 0
                for u in range(NX):
                    ref = gacc.at[(block // 2) % NZL, block % 2, u]
                    top = d * 32 + u * 8
                    put(ref, slice(row * 8, row * 8 + 8), out[top : top + 8, :LANES], again)
                    put(ref, slice(64 + row * 8, 72 + row * 8), out[top : top + 8, LANES:], again)
                    top = at * 32 + u * 8
                    at_row = 128 + row % 4 * 8
                    put(ref, slice(at_row, at_row + 8), part[top : top + 8], again or row >= 4)

    def send_core(k):
        return pltpu.make_async_remote_copy(
            src_ref=s1.at[k], dst_ref=r1.at[k], send_sem=c1s.at[k], recv_sem=c1r.at[k],
            device_id={"core": 1 - co}, device_id_type=pl.DeviceIdType.MESH,
        )

    pair = xx + 1 - 2 * (xx % 2)
    mirror = 3 - xx

    def partners(k):
        return (pair, mirror) if k < 3 else (mirror, pair)

    def second_of_first(k):
        first = partners(k)[0]
        return 3 - first if k < 3 else first + 1 - 2 * (first % 2)

    def send_x1(k):
        return pltpu.make_async_remote_copy(
            src_ref=s2.at[k], dst_ref=r2.at[k], send_sem=c2s.at[k], recv_sem=c2r.at[k],
            device_id={"x": partners(k)[0]}, device_id_type=pl.DeviceIdType.MESH,
        )

    def send_x2(k):
        return pltpu.make_async_remote_copy(
            src_ref=s3.at[k], dst_ref=r3.at[k], send_sem=c3s.at[k], recv_sem=c3r.at[k],
            device_id={"x": partners(k)[1]}, device_id_type=pl.DeviceIdType.MESH,
        )

    def y_copy(k, i, slot, src, t):
        return pltpu.make_async_remote_copy(
            src_ref=s4.at[k, src], dst_ref=r4.at[k, slot], send_sem=c4s.at[k, i],
            recv_sem=c4r.at[k, slot], device_id={"y": t}, device_id_type=pl.DeviceIdType.MESH,
        )

    def z_copy(k, h, slot):
        return pltpu.make_async_remote_copy(
            src_ref=s5.at[k], dst_ref=r5.at[slot], send_sem=c5s.at[k, h], recv_sem=c5r.at[slot],
            device_id={"zl": k, "zh": h}, device_id_type=pl.DeviceIdType.MESH,
        )

    forward = pltpu.make_async_remote_copy(
        src_ref=mine, dst_ref=before, send_sem=fsem.at[0], recv_sem=fsem.at[1],
        device_id={"x": jnp.minimum(xx + 1, NX - 1)}, device_id_type=pl.DeviceIdType.MESH,
    )

    def summed(k, u):
        return gacc[k, co, u] + r1[k, u].astype(f32)

    def step_x1(k):
        send_core(k).wait_recv()
        s2[k, 0] = summed(k, partners(k)[0]).astype(bf16)
        s2[k, 1] = summed(k, second_of_first(k)).astype(bf16)
        send_x1(k).start()

    def step_x2(k):
        send_x1(k).wait_recv()
        s3[k] = (summed(k, partners(k)[1]) + r2[k, 1].astype(f32)).astype(bf16)
        send_x2(k).start()

    def step_y(k):
        send_x2(k).wait_recv()
        val = summed(k, xx) + r2[k, 0].astype(f32) + r3[k].astype(f32)
        for i in range(2):
            bown[k, :, i * 8 : i * 8 + 8, :] = val[i * 64 : i * 64 + 64].reshape(NY, 8, LANES)
        rest = val[128:].reshape(NY // 2, 8, LANES)
        bown[k, : NY // 2, 16:, :] = rest
        bown[k, NY // 2 :, 16:, :] = rest
        s4[k] = bown[k].astype(bf16)

        def go(i, c):
            t = (yy + i) % NY
            y_copy(k, i, yy, t, t).start()
            return c

        lax.fori_loop(1, NY, go, 0)

    def step_z(k):
        def go(i, acc):
            t = (yy + i) % NY
            y_copy(k, i, t, t, t).wait_recv()
            return acc + r4[k, t].astype(f32)

        val = lax.fori_loop(1, NY, go, bown[k, yy])
        cown[k] = val
        s5[k] = val.astype(bf16)
        for h in range(NZH):
            @pl.when(jnp.logical_or(zl != k, zh != h))
            def _():
                z_copy(k, h, z12).start()

    for k in ORDER:
        s1[k] = gacc[k, 1 - co].astype(bf16)
        send_core(k).start()

    mean_n = column(row2, 2)
    square_n = column(row2, 3)
    rstd_n = lax.rsqrt(square_n - mean_n * mean_n + EPS)
    affine_n = (zn[...] - mean_n) * rstd_n * gam[...] + bet[...]
    y_next = (affine_n * jax.nn.sigmoid(affine_n)).astype(bf16)
    y_out[0, 0] = y_next[:, :COLS]
    y_out[0, 1] = y_next[:, COLS:]

    for k in ORDER:
        step_x1(k)

    for step in range(len(ORDER) + 2):
        if step < 6:
            step_x2(ORDER[step])
        if step >= 2:
            step_y(ORDER[step - 2])
    for k in ORDER:
        step_z(k)

    @pl.when(has_prev)
    def _():
        gz_next.wait_recv()

    @pl.when(jnp.logical_not(has_prev))
    def _():
        gzh[0] = jnp.zeros((CH, COLS), bf16)

    @pl.when(has_next)
    def _():
        gz_prev.wait_recv()

    @pl.when(jnp.logical_not(has_next))
    def _():
        gzh[1] = jnp.zeros((CH, COLS), bf16)

    put_shifts(gzs, 0, gzh[0])
    put_shifts(gzs, 1, gzo[0])
    put_shifts(gzs, 2, gzo[1])
    put_shifts(gzs, 3, gzh[1])
    zc[...] = jnp.zeros_like(zc)

    def back(t, c):
        a, b = t // 3, t % 3
        source = jnp.concatenate([gzs[2 - b, 2 - a, :CH], gzs[2 - b, 3 - a, :CH]], axis=1)
        zc[...] += dot(kv[a, b], source, TN)
        return c

    lax.fori_loop(0, 9, back, 0)
    grad_x = zc[...].astype(bf16)
    gx_out[0, 0] = grad_x[:, :COLS]
    gx_out[0, 1] = grad_x[:, COLS:]

    def gather_z(i, acc):
        t = (z12 + i) % NZ
        z_copy(0, 0, t).wait_recv()
        return acc + r5[t].astype(f32)

    mine[...] = lax.fori_loop(1, NZ, gather_z, cown[zl])

    @pl.when(xx < NX - 1)
    def _():
        forward.start()

    @pl.when(has_next)
    def _():
        halos[0].wait_send()
        halos[2].wait_send()
        gz_next.wait_send()

    @pl.when(has_prev)
    def _():
        halos[1].wait_send()
        halos[3].wait_send()
        gz_prev.wait_send()

    sent_all(a_copy, ra, as_, ar, m, NM)
    sent_all(b_copy, rb, bs, br, yy, NY)
    sent_all(a_copy, ra2, as2, ar2, m, NM)
    sent_all(b_copy, rb2, bs2, br2, yy, NY)
    for k in range(NZL):
        send_core(k).wait_send()
        send_x1(k).wait_send()
        send_x2(k).wait_send()

        def sent_y(i, c):
            y_copy(k, i, yy, (yy + i) % NY, (yy + i) % NY).wait_send()
            return c

        lax.fori_loop(1, NY, sent_y, 0)
        for h in range(NZH):
            @pl.when(jnp.logical_or(zl != k, zh != h))
            def _():
                z_copy(k, h, z12).wait_send()

    gk_out[0] = mine[...]

    @pl.when(xx > 0)
    def _():
        forward.wait_recv()

    @pl.when(xx == 0)
    def _():
        before[...] = jnp.zeros_like(before)

    gk_out[1] = before[...]

    @pl.when(xx < NX - 1)
    def _():
        forward.wait_send()


def last(y_in, gx_in, raw, y_out, gx_out, gk_out, rows, sem):
    back = [
        pltpu.make_async_copy(y_in, y_out, sem.at[0]),
        pltpu.make_async_copy(gx_in, gx_out, sem.at[1]),
    ]
    for cp in back:
        cp.start()
    second, high = lax.axis_index("zh") == 1, lax.axis_index("y") >= NY // 2
    for i in range(2):
        tile = raw[i]
        rest = tile[16:]
        parts = (tile[:8], tile[8:16], jnp.where(high, pltpu.roll(rest, REST, 1), rest))
        for t, p in enumerate(parts):
            four = jnp.where(second, p[4:], p[:4])
            lanes = slice(t * LANES, (t + 1) * LANES)
            if i == 0:
                rows[1:5, lanes] = four
            else:
                rows[0:1, lanes] = four[3:]
    share = 9 * CH * CH // (NH * NZH * NX)
    for v in range(NX):

        @pl.when(lax.axis_index("x") == v)
        def _():
            for start in range(0, share, LANES):
                n = min(LANES, share - start)
                r, col = divmod(share * v + start, CH)
                r = r - 4 * v + 1
                k = min(n, CH - col)
                piece = rows[r : r + 1, col : col + k]
                if k < n:
                    piece = jnp.concatenate([piece, rows[r + 1 : r + 2, : n - k]], axis=1)
                gk_out[pl.ds(start, n)] = piece.reshape(n)

    for cp in back:
        cp.wait()


def local(x_next, x_cur, grad_out, kernel, gamma, beta):
    vmem = pl.BlockSpec(memory_space=pltpu.VMEM)
    hbm = pl.BlockSpec(memory_space=pltpu.HBM)
    dma = pltpu.SemaphoreType.DMA
    V = pltpu.VMEM
    scratch = [
        V((CH,), f32), V((CH,), f32),
        V((4, CH, COLS), bf16), V((4, CH, COLS), bf16), V((2, CH, COLS), bf16),
        V((3, 3, CH, CH), bf16),
        V((3, 4, CH + REST, COLS), bf16), V((3, 4, 2 * REST, COLS), bf16), V((3, 4, CH, COLS), bf16),
        V((2, CH, COLS), bf16), V((2, CH, COLS), bf16), V((3, 4, CH, COLS), bf16),
        V((CH, 2 * COLS), f32), V((CH, 2 * COLS), f32), V((CH, 2 * COLS), f32), V((CH, 2 * COLS), f32),
        V((CH, COLS), f32), V((CH, 1), f32), V((CH, 1), f32),
        V((3, 32 * max(BLOCKS), CH), bf16),
        V((NM, 1, COLS), f32), V((NY, 1, COLS), f32), V((NM, 1, COLS), f32), V((NY, 1, COLS), f32),
        V((NZL, NC, NX, TALL, LANES), f32),
        V((NZL, NX, TALL, LANES), bf16), V((NZL, NX, TALL, LANES), bf16),
        V((NZL, 2, TALL, LANES), bf16), V((NZL, 2, TALL, LANES), bf16),
        V((NZL, TALL, LANES), bf16), V((NZL, TALL, LANES), bf16),
        V((NZL, NY, 24, LANES), bf16), V((NZL, NY, 24, LANES), bf16),
        V((NZL, NY, 24, LANES), f32),
        V((NZL, 24, LANES), bf16), V((NZL, 24, LANES), f32),
        V((NZ, 24, LANES), bf16), V((24, LANES), f32), V((24, LANES), f32),
        dma((6,)), dma((4,)), dma((4,)), dma((2,)), dma((2,)),
        dma((NM,)), dma((NM,)), dma((NY,)), dma((NY,)),
        dma((NM,)), dma((NM,)), dma((NY,)), dma((NY,)),
        dma((NZL,)), dma((NZL,)), dma((NZL,)), dma((NZL,)), dma((NZL,)), dma((NZL,)),
        dma((NZL, NY)), dma((NZL, NY)), dma((NZL, NZH)), dma((NZ,)), dma((2,)),
    ]
    y_next, grad_x, quarters = pl.pallas_call(
        body,
        out_shape=(
            pltpu.VMEM(x_next.shape, bf16),
            pltpu.VMEM(x_next.shape, bf16),
            pltpu.VMEM((2, 24, LANES), f32),
        ),
        in_specs=[hbm] * 6,
        out_specs=(vmem, vmem, vmem),
        scratch_shapes=scratch,
        compiler_params=pltpu.CompilerParams(
            collective_id=0, has_side_effects=True, vmem_limit_bytes=40 * 1024 * 1024
        ),
    )(*(pltpu.with_memory_space_constraint(v, pltpu.HBM) for v in (x_next, x_cur, grad_out, kernel, gamma, beta)))
    return pl.pallas_call(
        last,
        out_shape=(
            jax.ShapeDtypeStruct(x_next.shape, bf16),
            jax.ShapeDtypeStruct(x_next.shape, bf16),
            jax.ShapeDtypeStruct((9 * CH * CH // (NH * NZH * NX),), f32),
        ),
        in_specs=[vmem, vmem, vmem],
        out_specs=(hbm, hbm, vmem),
        scratch_shapes=[V((8, 3 * LANES), f32), dma((2,))],
        compiler_params=pltpu.CompilerParams(vmem_limit_bytes=8 * 1024 * 1024),
    )(y_next, grad_x, quarters)


def solution(mesh):
    torus = Mesh(mesh.devices.reshape(NY, NZL, NC, NZH, NX), HEIGHT + DP)
    image = P(DP, HEIGHT, None, None)
    return jax.shard_map(
        local,
        mesh=torus,
        in_specs=(image, image, image, P(), P(), P()),
        out_specs=(image, image, P(HEIGHT + DP)),
        check_vma=False,
    )
```

```python
import jax
import jax.numpy as jnp
from jax import lax
from jax.experimental import pallas as pl
from jax.experimental.pallas import tpu as pltpu
from jax.sharding import Mesh
from jax.sharding import PartitionSpec as P

CH = 320
COLS = 128
LANES = 128
MAIN = 256
REST = CH - MAIN
TALL = 160
GROUP = 10
NY, NZL, NC, NZH, NX = 8, 6, 2, 2, 4
NM = NZL * NC
NH = NY * NM
NZ = NZL * NZH
COUNT = 192 * GROUP * COLS
EPS = 1e-05
HEIGHT = ("y", "zl", "core")
DP = ("zh", "x")
FIRST = (0, 10, 21)
BLOCKS = (11, 12, 11)
ORDER = (0, 3, 1, 4, 2, 5)

f32 = jnp.float32
bf16 = jnp.bfloat16


def dot(a, b, dims=(((1,), (0,)), ((), ()))):
    return lax.dot_general(a, b, dims, preferred_element_type=f32)


NT = (((1,), (1,)), ((), ()))
TN = (((0,), (0,)), ((), ()))


def body(
    xn_in, xc_in, go_in, k_in, gam_in, bet_in,
    y_out, gx_out, gk_out,
    gam_row, bet_row, xcr, xnr, gor, kv, xcs, xhi, xns, gzo, gzh, gzs,
    zc, zn, nrm, gn, emask, gam, bet, selm,
    ra, rb, ra2, rb2,
    gacc, s1, r1, s2, r2, s3, r3, s4, r4, bown, s5, cown, r5, zown, s7, r7, mid, s8, r8, mine, before,
    lsem, hs, hr, ghs, ghr, as_, ar, bs, br, as2, ar2, bs2, br2,
    c1s, c1r, c2s, c2r, c3s, c3r, c4s, c4r, c5s, c5r, c7s, c7r, c8s, c8r, fsem,
):
    yy, zl, co = lax.axis_index("y"), lax.axis_index("zl"), lax.axis_index("core")
    zh, xx = lax.axis_index("zh"), lax.axis_index("x")
    m = zl * NC + co
    pos = yy * NM + m
    z12 = zl * NZH + zh

    def height_id(p):
        return {"y": p // NM, "zl": (p // NC) % NZL, "core": p % NC}

    has_prev, has_next = pos > 0, pos < NH - 1
    prev_id, next_id = height_id(jnp.maximum(pos - 1, 0)), height_id(jnp.minimum(pos + 1, NH - 1))

    barrier = pltpu.get_barrier_semaphore()

    def greet(device_id):
        pl.semaphore_signal(barrier, inc=1, device_id=device_id, device_id_type=pl.DeviceIdType.MESH)

    @pl.when(has_prev)
    def _():
        greet(prev_id)

    @pl.when(has_next)
    def _():
        greet(next_id)

    def far_z(i, c):
        greet({"zl": i, "zh": 1 - zh})
        return c

    lax.fori_loop(0, NZL, far_z, 0)

    def far_m(i, c):
        t = (m + i) % NM
        greet({"zl": t // NC, "core": t % NC})
        return c

    lax.fori_loop(1, NM, far_m, 0)

    def far_y(i, c):
        greet({"y": (yy + i) % NY})
        return c

    lax.fori_loop(1, NY, far_y, 0)

    def far_x(i, c):
        greet({"x": (xx + i) % NX})
        return c

    lax.fori_loop(1, NX, far_x, 0)

    cp_xc = pltpu.make_async_copy(xc_in.at[0], xcr.at[pl.ds(1, 2)], lsem.at[0])
    cp_k = pltpu.make_async_copy(k_in, kv, lsem.at[1])
    cp_xn = pltpu.make_async_copy(xn_in.at[0], xnr.at[pl.ds(1, 2)], lsem.at[2])
    cp_go = pltpu.make_async_copy(go_in.at[0], gor, lsem.at[3])
    cp_gam = pltpu.make_async_copy(gam_in, gam_row, lsem.at[4])
    cp_bet = pltpu.make_async_copy(bet_in, bet_row, lsem.at[5])
    for cp in (cp_xc, cp_gam, cp_bet, cp_k, cp_xn, cp_go):
        cp.start()

    greeted = NZL + (NM - 1) + (NY - 1) + (NX - 1)
    pl.semaphore_wait(barrier, greeted + has_prev.astype(jnp.int32) + has_next.astype(jnp.int32))

    def halo(src, dst, to_next, i, send, recv):
        return pltpu.make_async_remote_copy(
            src_ref=src.at[0, 1] if to_next else src.at[0, 0],
            dst_ref=dst.at[0] if to_next else dst.at[3],
            send_sem=send.at[i],
            recv_sem=recv.at[i],
            device_id=next_id if to_next else prev_id,
            device_id_type=pl.DeviceIdType.MESH,
        )

    halos = (
        halo(xc_in, xcr, True, 0, hs, hr),
        halo(xc_in, xcr, False, 1, hs, hr),
        halo(xn_in, xnr, True, 2, hs, hr),
        halo(xn_in, xnr, False, 3, hs, hr),
    )

    @pl.when(has_next)
    def _():
        halos[0].start()

    @pl.when(has_prev)
    def _():
        halos[1].start()

    rows_i = lax.broadcasted_iota(jnp.int32, (CH, COLS), 0)
    lane_i = lax.broadcasted_iota(jnp.int32, (CH, COLS), 1)
    rel = rows_i - GROUP * (lane_i & 31)
    emask[...] = jnp.where((rel >= 0) & (rel < GROUP), 1.0, 0.0).astype(f32)
    eye = lax.broadcasted_iota(jnp.int32, (CH, CH), 0) == lax.broadcasted_iota(jnp.int32, (CH, CH), 1)
    cp_gam.wait()
    cp_bet.wait()
    gam[...] = jnp.sum(jnp.where(eye, gam_row[...].reshape(1, CH), 0.0), axis=1, keepdims=True)
    bet[...] = jnp.sum(jnp.where(eye, bet_row[...].reshape(1, CH), 0.0), axis=1, keepdims=True)
    zc[...] = jnp.zeros_like(zc)
    zn[...] = jnp.zeros_like(zn)
    for b in range(3):
        for r in range(4):
            xcs[b, r, CH:, :] = jnp.zeros((REST, COLS), bf16)
            xhi[b, r, :REST, :] = jnp.zeros((REST, COLS), bf16)

    lane = lax.broadcasted_iota(jnp.int32, (CH, COLS), 1)

    def put_shifts(dst, row, v, high=None):
        wide = v.astype(f32)
        moved = (
            jnp.where(lane == 0, 0.0, pltpu.roll(wide, 1, 1)).astype(bf16),
            v,
            jnp.where(lane == COLS - 1, 0.0, pltpu.roll(wide, COLS - 1, 1)).astype(bf16),
        )
        for b in range(3):
            dst[b, row, :CH, :] = moved[b]
            if high is not None:
                high[b, row, REST:, :] = moved[b][MAIN:]

    cp_xc.wait()
    put_shifts(xcs, 1, xcr[1], xhi)
    put_shifts(xcs, 2, xcr[2], xhi)

    cp_k.wait()

    def conv_inner(acc, xs):
        def go(b, c):
            x1, x2 = xs[b, 1, :CH], xs[b, 2, :CH]
            acc[...] += dot(kv[1, b], jnp.concatenate([x1, x2], axis=1))
            acc[:, COLS:] += dot(kv[0, b], x1)
            acc[:, :COLS] += dot(kv[2, b], x2)
            return c

        lax.fori_loop(0, 3, go, 0)

    def conv_outer(acc, xs):
        def go(b, c):
            acc[:, :COLS] += dot(kv[0, b], xs[b, 0, :CH])
            acc[:, COLS:] += dot(kv[2, b], xs[b, 3, :CH])
            return c

        lax.fori_loop(0, 3, go, 0)

    conv_inner(zc, xcs)

    for b in range(3):
        n = BLOCKS[b] * 32
        rho = lax.broadcasted_iota(jnp.int32, (n, CH), 0)
        col = lax.broadcasted_iota(jnp.int32, (n, CH), 1)
        part = ((rho >> 3) & 3) * 4 + (rho & 3)
        src = 30 * (FIRST[b] + (rho >> 5)) + 15 * ((rho >> 2) & 1) + part - CH * b
        selm[b, :n, :] = jnp.where((part < 15) & (src == col), 1.0, 0.0).astype(bf16)

    def halo_wait(raw, up, down):
        @pl.when(has_prev)
        def _():
            up.wait_recv()

        @pl.when(jnp.logical_not(has_prev))
        def _():
            raw[0] = jnp.zeros((CH, COLS), bf16)

        @pl.when(has_next)
        def _():
            down.wait_recv()

        @pl.when(jnp.logical_not(has_next))
        def _():
            raw[3] = jnp.zeros((CH, COLS), bf16)

    halo_wait(xcr, halos[0], halos[1])

    @pl.when(has_next)
    def _():
        halos[2].start()

    @pl.when(has_prev)
    def _():
        halos[3].start()

    put_shifts(xcs, 0, xcr[0], xhi)
    put_shifts(xcs, 3, xcr[3], xhi)
    conv_outer(zc, xcs)

    def tile_of(cols4):
        q = lane >> 5
        picked = jnp.zeros((CH, COLS), f32)
        for i, v in enumerate(cols4):
            picked = jnp.where(q == i, v, picked)
        return jnp.sum(picked * emask[...], axis=0, keepdims=True)

    def a_copy(buf, send, recv, i, slot, t):
        return pltpu.make_async_remote_copy(
            src_ref=buf.at[slot],
            dst_ref=buf.at[slot],
            send_sem=send.at[i],
            recv_sem=recv.at[slot],
            device_id={"zl": t // NC, "core": t % NC},
            device_id_type=pl.DeviceIdType.MESH,
        )

    def b_copy(buf, send, recv, i, slot, t):
        return pltpu.make_async_remote_copy(
            src_ref=buf.at[slot],
            dst_ref=buf.at[slot],
            send_sem=send.at[i],
            recv_sem=recv.at[slot],
            device_id={"y": t},
            device_id_type=pl.DeviceIdType.MESH,
        )

    def start_all(copy, buf, send, recv, me, n, tile):
        buf[me] = tile

        def go(i, c):
            copy(buf, send, recv, i, me, (me + i) % n).start()
            return c

        lax.fori_loop(1, n, go, 0)

    def wait_all(copy, buf, send, recv, me, n):
        def go(i, c):
            t = (me + i) % n
            copy(buf, send, recv, i, t, t).wait_recv()
            return c

        lax.fori_loop(1, n, go, 0)
        return jnp.sum(buf[...], axis=0)

    def sent_all(copy, buf, send, recv, me, n):
        def go(i, c):
            copy(buf, send, recv, i, me, (me + i) % n).wait_send()
            return c

        lax.fori_loop(1, n, go, 0)

    z = zc[...]
    start_all(
        a_copy, ra, as_, ar, m, NM,
        tile_of((jnp.sum(z, axis=1, keepdims=True), jnp.sum(z * z, axis=1, keepdims=True))),
    )

    cp_xn.wait()
    put_shifts(xns, 1, xnr[1])
    put_shifts(xns, 2, xnr[2])
    conv_inner(zn, xns)
    start_all(b_copy, rb, bs, br, yy, NY, wait_all(a_copy, ra, as_, ar, m, NM))
    halo_wait(xnr, halos[2], halos[3])
    put_shifts(xns, 0, xnr[0])
    put_shifts(xns, 3, xnr[3])
    conv_outer(zn, xns)
    zv = zn[...]
    next_sums = (jnp.sum(zv, axis=1, keepdims=True), jnp.sum(zv * zv, axis=1, keepdims=True))
    cp_go.wait()
    total = wait_all(b_copy, rb, bs, br, yy, NY)

    def column(row, block):
        keep = (lane >> 5) == block
        return jnp.sum(jnp.where(keep, emask[...] * row, 0.0), axis=1, keepdims=True)

    def moments(tile, first):
        row = tile / COUNT
        mean_row = pltpu.roll(jnp.broadcast_to(row, (8, COLS)), (128 - 32 * first) % 128, 1)[:1]
        square_row = pltpu.roll(jnp.broadcast_to(row, (8, COLS)), (128 - 32 * (first + 1)) % 128, 1)[:1]
        rstd_row = lax.rsqrt(square_row - mean_row * mean_row + EPS)
        return column(mean_row, 0), column(rstd_row, 0)

    mean_c, rstd_c = moments(total, 0)
    normed = (zc[...] - mean_c) * rstd_c
    nrm[...] = normed
    affine = normed * gam[...] + bet[...]
    sig = jax.nn.sigmoid(affine)
    grad = jnp.concatenate([gor[0], gor[1]], axis=1).astype(f32)
    grad_n = grad * (sig * (1.0 + affine * (1.0 - sig))) * gam[...]
    gn[...] = grad_n
    start_all(
        a_copy, ra2, as2, ar2, m, NM,
        tile_of(
            (
                jnp.sum(grad_n, axis=1, keepdims=True),
                jnp.sum(grad_n * normed, axis=1, keepdims=True),
            )
            + next_sums
        ),
    )
    start_all(b_copy, rb2, bs2, br2, yy, NY, wait_all(a_copy, ra2, as2, ar2, m, NM))
    total2 = wait_all(b_copy, rb2, bs2, br2, yy, NY)
    row2 = total2 / COUNT
    mean_1, mean_2 = column(row2, 0), column(row2, 1)
    gz = (rstd_c * (gn[...] - mean_1 - nrm[...] * mean_2)).astype(bf16)
    gzo[0] = gz[:, :COLS]
    gzo[1] = gz[:, COLS:]

    def gz_copy(to_next):
        return pltpu.make_async_remote_copy(
            src_ref=gzo.at[1] if to_next else gzo.at[0],
            dst_ref=gzh.at[0] if to_next else gzh.at[1],
            send_sem=ghs.at[0 if to_next else 1],
            recv_sem=ghr.at[0 if to_next else 1],
            device_id=next_id if to_next else prev_id,
            device_id_type=pl.DeviceIdType.MESH,
        )

    gz_next, gz_prev = gz_copy(True), gz_copy(False)

    @pl.when(has_next)
    def _():
        gz_next.start()

    @pl.when(has_prev)
    def _():
        gz_prev.start()

    picked = [dot(selm[b, : BLOCKS[b] * 32], gz).astype(bf16) for b in range(3)]

    def put(ref, rows, piece, add):
        if add:
            ref[rows, :] += piece
        else:
            ref[rows, :] = piece

    for a in range(3):
        for b in range(3):
            first = 32 * a + FIRST[b]
            low = min(max(NH // 2 - first, 0), BLOCKS[b])
            out = dot(picked[b], jnp.concatenate([xcs[b, a, :MAIN], xcs[b, a + 1, :MAIN]], axis=1), NT)
            rest = []
            if low > 0:
                source = jnp.concatenate([xcs[b, a, MAIN:], xcs[b, a + 1, MAIN:]], axis=1)
                rest.append(dot(picked[b][: low * 32], source, NT))
            if low < BLOCKS[b]:
                source = jnp.concatenate([xhi[b, a], xhi[b, a + 1]], axis=1)
                rest.append(dot(picked[b][low * 32 :], source, NT))
            for d in range(BLOCKS[b]):
                block = first + d
                row = block // NM
                part, at = (rest[0], d) if d < low else (rest[-1], d - low)
                again = d == 0 and b > 0
                for u in range(NX):
                    ref = gacc.at[(block // 2) % NZL, block % 2, u]
                    top = d * 32 + u * 8
                    put(ref, slice(row * 8, row * 8 + 8), out[top : top + 8, :LANES], again)
                    put(ref, slice(64 + row * 8, 72 + row * 8), out[top : top + 8, LANES:], again)
                    top = at * 32 + u * 8
                    at_row = 128 + row % 4 * 8
                    put(ref, slice(at_row, at_row + 8), part[top : top + 8], again or row >= 4)

    def send_core(k):
        return pltpu.make_async_remote_copy(
            src_ref=s1.at[k], dst_ref=r1.at[k], send_sem=c1s.at[k], recv_sem=c1r.at[k],
            device_id={"core": 1 - co}, device_id_type=pl.DeviceIdType.MESH,
        )

    pair = xx + 1 - 2 * (xx % 2)
    mirror = 3 - xx

    def partners(k):
        return (pair, mirror) if k < 3 else (mirror, pair)

    def second_of_first(k):
        first = partners(k)[0]
        return 3 - first if k < 3 else first + 1 - 2 * (first % 2)

    def send_x1(k):
        return pltpu.make_async_remote_copy(
            src_ref=s2.at[k], dst_ref=r2.at[k], send_sem=c2s.at[k], recv_sem=c2r.at[k],
            device_id={"x": partners(k)[0]}, device_id_type=pl.DeviceIdType.MESH,
        )

    def send_x2(k):
        return pltpu.make_async_remote_copy(
            src_ref=s3.at[k], dst_ref=r3.at[k], send_sem=c3s.at[k], recv_sem=c3r.at[k],
            device_id={"x": partners(k)[1]}, device_id_type=pl.DeviceIdType.MESH,
        )

    def y_copy(k, i, slot, src, t):
        return pltpu.make_async_remote_copy(
            src_ref=s4.at[k, src], dst_ref=r4.at[k, slot], send_sem=c4s.at[k, i],
            recv_sem=c4r.at[k, slot], device_id={"y": t}, device_id_type=pl.DeviceIdType.MESH,
        )

    def z_copy(k, h, slot):
        return pltpu.make_async_remote_copy(
            src_ref=s5.at[k], dst_ref=r5.at[slot], send_sem=c5s.at[k, h], recv_sem=c5r.at[slot],
            device_id={"zl": k, "zh": h}, device_id_type=pl.DeviceIdType.MESH,
        )

    def z_first(k, h, slot):
        return pltpu.make_async_remote_copy(
            src_ref=s7.at[k, h], dst_ref=r7.at[slot], send_sem=c7s.at[k, h], recv_sem=c7r.at[slot],
            device_id={"zl": k, "zh": h}, device_id_type=pl.DeviceIdType.MESH,
        )

    def y_second(i, slot, t):
        return pltpu.make_async_remote_copy(
            src_ref=s8.at[t // 2], dst_ref=r8.at[slot], send_sem=c8s.at[i], recv_sem=c8r.at[slot],
            device_id={"y": t}, device_id_type=pl.DeviceIdType.MESH,
        )

    forward = pltpu.make_async_remote_copy(
        src_ref=mine, dst_ref=before, send_sem=fsem.at[0], recv_sem=fsem.at[1],
        device_id={"x": jnp.minimum(xx + 1, NX - 1)}, device_id_type=pl.DeviceIdType.MESH,
    )

    def summed(k, u):
        return gacc[k, co, u] + r1[k, u].astype(f32)

    def step_x1(k):
        send_core(k).wait_recv()
        s2[k, 0] = summed(k, partners(k)[0]).astype(bf16)
        s2[k, 1] = summed(k, second_of_first(k)).astype(bf16)
        send_x1(k).start()

    def step_x2(k):
        send_x1(k).wait_recv()
        s3[k] = (summed(k, partners(k)[1]) + r2[k, 1].astype(f32)).astype(bf16)
        send_x2(k).start()

    def step_y(k):
        send_x2(k).wait_recv()
        val = summed(k, xx) + r2[k, 0].astype(f32) + r3[k].astype(f32)
        bown[k, :, :8, :] = val[:64].reshape(NY, 8, LANES)
        rest = val[128:].reshape(NY // 2, 8, LANES)
        bown[k, : NY // 2, 8:, :] = rest
        bown[k, NY // 2 :, 8:, :] = rest
        s4[k] = bown[k].astype(bf16)
        for t in range(NY):
            for h in range(NZH):
                top = 64 + t * 8 + h * 4
                zown[k, h, t * 4 : t * 4 + 4, :] = val[top : top + 4]
        s7[k] = zown[k].astype(bf16)

        def go(i, c):
            t = (yy + i) % NY
            y_copy(k, i, yy, t, t).start()
            return c

        lax.fori_loop(1, NY, go, 0)
        for h in range(NZH):

            @pl.when(jnp.logical_or(zl != k, zh != h))
            def _():
                z_first(k, h, z12).start()

    def middle():
        def take(i, acc):
            t = (z12 + i) % NZ
            z_first(0, 0, t).wait_recv()
            return acc + r7[t].astype(f32)

        val = lax.fori_loop(1, NZ, take, zown[zl, zh]).reshape(NY // 2, 8, LANES)
        mid[...] = val
        s8[...] = val.astype(bf16)

        def go(i, c):
            t = (yy + i) % NY
            y_second(i, yy, t).start()
            return c

        lax.fori_loop(1, NY, go, 0)

    def middle_end():
        def go(i, acc):
            t = (yy + i) % NY
            y_second(i, t, t).wait_recv()
            return acc + r8[t].astype(f32)

        return lax.fori_loop(1, NY, go, mid[yy // 2])

    def step_z(k):
        def go(i, acc):
            t = (yy + i) % NY
            y_copy(k, i, t, t, t).wait_recv()
            return acc + r4[k, t].astype(f32)

        val = lax.fori_loop(1, NY, go, bown[k, yy])
        cown[k] = val
        s5[k] = val.astype(bf16)
        for h in range(NZH):
            @pl.when(jnp.logical_or(zl != k, zh != h))
            def _():
                z_copy(k, h, z12).start()

    for k in ORDER:
        s1[k] = gacc[k, 1 - co].astype(bf16)
        send_core(k).start()

    mean_n = column(row2, 2)
    square_n = column(row2, 3)
    rstd_n = lax.rsqrt(square_n - mean_n * mean_n + EPS)
    affine_n = (zn[...] - mean_n) * rstd_n * gam[...] + bet[...]
    y_next = (affine_n * jax.nn.sigmoid(affine_n)).astype(bf16)
    y_out[0, 0] = y_next[:, :COLS]
    y_out[0, 1] = y_next[:, COLS:]

    for k in ORDER:
        step_x1(k)

    for step in range(len(ORDER) + 2):
        if step < 6:
            step_x2(ORDER[step])
        if step >= 2:
            step_y(ORDER[step - 2])
    for k in ORDER:
        step_z(k)
    middle()

    @pl.when(has_prev)
    def _():
        gz_next.wait_recv()

    @pl.when(jnp.logical_not(has_prev))
    def _():
        gzh[0] = jnp.zeros((CH, COLS), bf16)

    @pl.when(has_next)
    def _():
        gz_prev.wait_recv()

    @pl.when(jnp.logical_not(has_next))
    def _():
        gzh[1] = jnp.zeros((CH, COLS), bf16)

    put_shifts(gzs, 0, gzh[0])
    put_shifts(gzs, 1, gzo[0])
    put_shifts(gzs, 2, gzo[1])
    put_shifts(gzs, 3, gzh[1])
    zc[...] = jnp.zeros_like(zc)

    def back(t, c):
        a, b = t // 3, t % 3
        source = jnp.concatenate([gzs[2 - b, 2 - a, :CH], gzs[2 - b, 3 - a, :CH]], axis=1)
        zc[...] += dot(kv[a, b], source, TN)
        return c

    lax.fori_loop(0, 9, back, 0)
    grad_x = zc[...].astype(bf16)
    gx_out[0, 0] = grad_x[:, :COLS]
    gx_out[0, 1] = grad_x[:, COLS:]

    def gather_z(i, acc):
        t = (z12 + i) % NZ
        z_copy(0, 0, t).wait_recv()
        return acc + r5[t].astype(f32)

    total_z = lax.fori_loop(1, NZ, gather_z, cown[zl])
    mine[:8] = total_z[:8]
    mine[8:16] = middle_end()
    mine[16:] = total_z[8:]

    @pl.when(xx < NX - 1)
    def _():
        forward.start()

    @pl.when(has_next)
    def _():
        halos[0].wait_send()
        halos[2].wait_send()
        gz_next.wait_send()

    @pl.when(has_prev)
    def _():
        halos[1].wait_send()
        halos[3].wait_send()
        gz_prev.wait_send()

    sent_all(a_copy, ra, as_, ar, m, NM)
    sent_all(b_copy, rb, bs, br, yy, NY)
    sent_all(a_copy, ra2, as2, ar2, m, NM)
    sent_all(b_copy, rb2, bs2, br2, yy, NY)
    for k in range(NZL):
        send_core(k).wait_send()
        send_x1(k).wait_send()
        send_x2(k).wait_send()

        def sent_y(i, c):
            y_copy(k, i, yy, (yy + i) % NY, (yy + i) % NY).wait_send()
            return c

        lax.fori_loop(1, NY, sent_y, 0)
        for h in range(NZH):
            @pl.when(jnp.logical_or(zl != k, zh != h))
            def _():
                z_copy(k, h, z12).wait_send()
                z_first(k, h, z12).wait_send()

    def sent_second(i, c):
        y_second(i, yy, (yy + i) % NY).wait_send()
        return c

    lax.fori_loop(1, NY, sent_second, 0)
    gk_out[0] = mine[...]

    @pl.when(xx > 0)
    def _():
        forward.wait_recv()

    @pl.when(xx == 0)
    def _():
        before[...] = jnp.zeros_like(before)

    gk_out[1] = before[...]

    @pl.when(xx < NX - 1)
    def _():
        forward.wait_send()


def last(y_in, gx_in, raw, y_out, gx_out, gk_out, rows, sem):
    back = [
        pltpu.make_async_copy(y_in, y_out, sem.at[0]),
        pltpu.make_async_copy(gx_in, gx_out, sem.at[1]),
    ]
    for cp in back:
        cp.start()
    second, high = lax.axis_index("zh") == 1, lax.axis_index("y") >= NY // 2
    odd = lax.axis_index("y") % 2 == 1
    for i in range(2):
        tile = raw[i]
        rest = tile[16:]
        parts = (tile[:8], tile[8:16], jnp.where(high, pltpu.roll(rest, REST, 1), rest))
        for t, p in enumerate(parts):
            four = jnp.where(odd if t == 1 else second, p[4:], p[:4])
            lanes = slice(t * LANES, (t + 1) * LANES)
            if i == 0:
                rows[1:5, lanes] = four
            else:
                rows[0:1, lanes] = four[3:]
    share = 9 * CH * CH // (NH * NZH * NX)
    for v in range(NX):

        @pl.when(lax.axis_index("x") == v)
        def _():
            for start in range(0, share, LANES):
                n = min(LANES, share - start)
                r, col = divmod(share * v + start, CH)
                r = r - 4 * v + 1
                k = min(n, CH - col)
                piece = rows[r : r + 1, col : col + k]
                if k < n:
                    piece = jnp.concatenate([piece, rows[r + 1 : r + 2, : n - k]], axis=1)
                gk_out[pl.ds(start, n)] = piece.reshape(n)

    for cp in back:
        cp.wait()


def local(x_next, x_cur, grad_out, kernel, gamma, beta):
    vmem = pl.BlockSpec(memory_space=pltpu.VMEM)
    hbm = pl.BlockSpec(memory_space=pltpu.HBM)
    dma = pltpu.SemaphoreType.DMA
    V = pltpu.VMEM
    scratch = [
        V((CH,), f32), V((CH,), f32),
        V((4, CH, COLS), bf16), V((4, CH, COLS), bf16), V((2, CH, COLS), bf16),
        V((3, 3, CH, CH), bf16),
        V((3, 4, CH + REST, COLS), bf16), V((3, 4, 2 * REST, COLS), bf16), V((3, 4, CH, COLS), bf16),
        V((2, CH, COLS), bf16), V((2, CH, COLS), bf16), V((3, 4, CH, COLS), bf16),
        V((CH, 2 * COLS), f32), V((CH, 2 * COLS), f32), V((CH, 2 * COLS), f32), V((CH, 2 * COLS), f32),
        V((CH, COLS), f32), V((CH, 1), f32), V((CH, 1), f32),
        V((3, 32 * max(BLOCKS), CH), bf16),
        V((NM, 1, COLS), f32), V((NY, 1, COLS), f32), V((NM, 1, COLS), f32), V((NY, 1, COLS), f32),
        V((NZL, NC, NX, TALL, LANES), f32),
        V((NZL, NX, TALL, LANES), bf16), V((NZL, NX, TALL, LANES), bf16),
        V((NZL, 2, TALL, LANES), bf16), V((NZL, 2, TALL, LANES), bf16),
        V((NZL, TALL, LANES), bf16), V((NZL, TALL, LANES), bf16),
        V((NZL, NY, 16, LANES), bf16), V((NZL, NY, 16, LANES), bf16),
        V((NZL, NY, 16, LANES), f32),
        V((NZL, 16, LANES), bf16), V((NZL, 16, LANES), f32),
        V((NZ, 16, LANES), bf16),
        V((NZL, NZH, NY * 4, LANES), f32), V((NZL, NZH, NY * 4, LANES), bf16), V((NZ, NY * 4, LANES), bf16),
        V((NY // 2, 8, LANES), f32), V((NY // 2, 8, LANES), bf16), V((NY, 8, LANES), bf16),
        V((24, LANES), f32), V((24, LANES), f32),
        dma((6,)), dma((4,)), dma((4,)), dma((2,)), dma((2,)),
        dma((NM,)), dma((NM,)), dma((NY,)), dma((NY,)),
        dma((NM,)), dma((NM,)), dma((NY,)), dma((NY,)),
        dma((NZL,)), dma((NZL,)), dma((NZL,)), dma((NZL,)), dma((NZL,)), dma((NZL,)),
        dma((NZL, NY)), dma((NZL, NY)), dma((NZL, NZH)), dma((NZ,)),
        dma((NZL, NZH)), dma((NZ,)), dma((NY,)), dma((NY,)), dma((2,)),
    ]
    y_next, grad_x, quarters = pl.pallas_call(
        body,
        out_shape=(
            pltpu.VMEM(x_next.shape, bf16),
            pltpu.VMEM(x_next.shape, bf16),
            pltpu.VMEM((2, 24, LANES), f32),
        ),
        in_specs=[hbm] * 6,
        out_specs=(vmem, vmem, vmem),
        scratch_shapes=scratch,
        compiler_params=pltpu.CompilerParams(
            collective_id=0, has_side_effects=True, vmem_limit_bytes=40 * 1024 * 1024
        ),
    )(*(pltpu.with_memory_space_constraint(v, pltpu.HBM) for v in (x_next, x_cur, grad_out, kernel, gamma, beta)))
    return pl.pallas_call(
        last,
        out_shape=(
            jax.ShapeDtypeStruct(x_next.shape, bf16),
            jax.ShapeDtypeStruct(x_next.shape, bf16),
            jax.ShapeDtypeStruct((9 * CH * CH // (NH * NZH * NX),), f32),
        ),
        in_specs=[vmem, vmem, vmem],
        out_specs=(hbm, hbm, vmem),
        scratch_shapes=[V((8, 3 * LANES), f32), dma((2,))],
        compiler_params=pltpu.CompilerParams(vmem_limit_bytes=8 * 1024 * 1024),
    )(y_next, grad_x, quarters)


def solution(mesh):
    torus = Mesh(mesh.devices.reshape(NY, NZL, NC, NZH, NX), HEIGHT + DP)
    image = P(DP, HEIGHT, None, None)
    return jax.shard_map(
        local,
        mesh=torus,
        in_specs=(image, image, image, P(), P(), P()),
        out_specs=(image, image, P(HEIGHT + DP)),
        check_vma=False,
    )
```

```python
import jax
import jax.numpy as jnp
from jax import lax
from jax.experimental import pallas as pl
from jax.experimental.pallas import tpu as pltpu
from jax.sharding import Mesh
from jax.sharding import PartitionSpec as P

CH = 320
COLS = 128
LANES = 128
MAIN = 256
REST = CH - MAIN
TALL = 160
GROUP = 10
NY, NZL, NC, NZH, NX = 8, 6, 2, 2, 4
NM = NZL * NC
NH = NY * NM
NZ = NZL * NZH
COUNT = 192 * GROUP * COLS
EPS = 1e-05
HEIGHT = ("y", "zl", "core")
DP = ("zh", "x")
FIRST = (0, 10, 21)
BLOCKS = (11, 12, 11)
ORDER = (0, 3, 1, 4, 2, 5)

f32 = jnp.float32
bf16 = jnp.bfloat16


def dot(a, b, dims=(((1,), (0,)), ((), ()))):
    return lax.dot_general(a, b, dims, preferred_element_type=f32)


NT = (((1,), (1,)), ((), ()))
TN = (((0,), (0,)), ((), ()))


def body(
    xn_in, xc_in, go_in, k_in, gam_in, bet_in,
    y_out, gx_out, gk_out,
    gam_row, bet_row, xcr, xnr, gor, kv, xcs, xhi, xns, gzo, gzh, gzs,
    zc, zn, nrm, gn, emask, gam, bet, selm,
    ra, rb, ra2, rb2,
    gacc, s1, r1, s2, r2, s3, r3, s4, r4, bown, s5, cown, r5, zown, s7, r7, mid, s8, r8, mine, before,
    lsem, hs, hr, ghs, ghr, as_, ar, bs, br, as2, ar2, bs2, br2,
    c1s, c1r, c2s, c2r, c3s, c3r, c4s, c4r, c5s, c5r, c7s, c7r, c8s, c8r, fsem,
):
    yy, zl, co = lax.axis_index("y"), lax.axis_index("zl"), lax.axis_index("core")
    zh, xx = lax.axis_index("zh"), lax.axis_index("x")
    m = zl * NC + co
    pos = yy * NM + m
    z12 = zl * NZH + zh

    def height_id(p):
        return {"y": p // NM, "zl": (p // NC) % NZL, "core": p % NC}

    has_prev, has_next = pos > 0, pos < NH - 1
    prev_id, next_id = height_id(jnp.maximum(pos - 1, 0)), height_id(jnp.minimum(pos + 1, NH - 1))

    barrier = pltpu.get_barrier_semaphore()

    def greet(device_id):
        pl.semaphore_signal(barrier, inc=1, device_id=device_id, device_id_type=pl.DeviceIdType.MESH)

    @pl.when(has_prev)
    def _():
        greet(prev_id)

    @pl.when(has_next)
    def _():
        greet(next_id)

    def far_z(i, c):
        greet({"zl": i, "zh": 1 - zh})
        return c

    lax.fori_loop(0, NZL, far_z, 0)

    def far_m(i, c):
        t = (m + i) % NM
        greet({"zl": t // NC, "core": t % NC})
        return c

    lax.fori_loop(1, NM, far_m, 0)

    def far_y(i, c):
        greet({"y": (yy + i) % NY})
        return c

    lax.fori_loop(1, NY, far_y, 0)

    def far_x(i, c):
        greet({"x": (xx + i) % NX})
        return c

    lax.fori_loop(1, NX, far_x, 0)

    cp_xc = pltpu.make_async_copy(xc_in.at[0], xcr.at[pl.ds(1, 2)], lsem.at[0])
    cp_k = pltpu.make_async_copy(k_in, kv, lsem.at[1])
    cp_xn = pltpu.make_async_copy(xn_in.at[0], xnr.at[pl.ds(1, 2)], lsem.at[2])
    cp_go = pltpu.make_async_copy(go_in.at[0], gor, lsem.at[3])
    cp_gam = pltpu.make_async_copy(gam_in, gam_row, lsem.at[4])
    cp_bet = pltpu.make_async_copy(bet_in, bet_row, lsem.at[5])
    for cp in (cp_xc, cp_gam, cp_bet, cp_k, cp_xn, cp_go):
        cp.start()

    greeted = NZL + (NM - 1) + (NY - 1) + (NX - 1)
    pl.semaphore_wait(barrier, greeted + has_prev.astype(jnp.int32) + has_next.astype(jnp.int32))

    def halo(src, dst, to_next, i, send, recv):
        return pltpu.make_async_remote_copy(
            src_ref=src.at[0, 1] if to_next else src.at[0, 0],
            dst_ref=dst.at[0] if to_next else dst.at[3],
            send_sem=send.at[i],
            recv_sem=recv.at[i],
            device_id=next_id if to_next else prev_id,
            device_id_type=pl.DeviceIdType.MESH,
        )

    halos = (
        halo(xc_in, xcr, True, 0, hs, hr),
        halo(xc_in, xcr, False, 1, hs, hr),
        halo(xn_in, xnr, True, 2, hs, hr),
        halo(xn_in, xnr, False, 3, hs, hr),
    )

    @pl.when(has_next)
    def _():
        halos[0].start()

    @pl.when(has_prev)
    def _():
        halos[1].start()

    rows_i = lax.broadcasted_iota(jnp.int32, (CH, COLS), 0)
    lane_i = lax.broadcasted_iota(jnp.int32, (CH, COLS), 1)
    rel = rows_i - GROUP * (lane_i & 31)
    emask[...] = jnp.where((rel >= 0) & (rel < GROUP), 1.0, 0.0).astype(f32)
    eye = lax.broadcasted_iota(jnp.int32, (CH, CH), 0) == lax.broadcasted_iota(jnp.int32, (CH, CH), 1)
    cp_gam.wait()
    cp_bet.wait()
    gam[...] = jnp.sum(jnp.where(eye, gam_row[...].reshape(1, CH), 0.0), axis=1, keepdims=True)
    bet[...] = jnp.sum(jnp.where(eye, bet_row[...].reshape(1, CH), 0.0), axis=1, keepdims=True)
    zc[...] = jnp.zeros_like(zc)
    zn[...] = jnp.zeros_like(zn)
    for b in range(3):
        for r in range(4):
            xcs[b, r, CH:, :] = jnp.zeros((REST, COLS), bf16)
            xhi[b, r, :REST, :] = jnp.zeros((REST, COLS), bf16)

    lane = lax.broadcasted_iota(jnp.int32, (CH, COLS), 1)

    def put_shifts(dst, row, v, high=None):
        wide = v.astype(f32)
        moved = (
            jnp.where(lane == 0, 0.0, pltpu.roll(wide, 1, 1)).astype(bf16),
            v,
            jnp.where(lane == COLS - 1, 0.0, pltpu.roll(wide, COLS - 1, 1)).astype(bf16),
        )
        for b in range(3):
            dst[b, row, :CH, :] = moved[b]
            if high is not None:
                high[b, row, REST:, :] = moved[b][MAIN:]

    cp_xc.wait()
    put_shifts(xcs, 1, xcr[1], xhi)
    put_shifts(xcs, 2, xcr[2], xhi)

    cp_k.wait()

    def conv_inner(acc, xs):
        def go(b, c):
            x1, x2 = xs[b, 1, :CH], xs[b, 2, :CH]
            acc[...] += dot(kv[1, b], jnp.concatenate([x1, x2], axis=1))
            acc[:, COLS:] += dot(kv[0, b], x1)
            acc[:, :COLS] += dot(kv[2, b], x2)
            return c

        lax.fori_loop(0, 3, go, 0)

    def conv_outer(acc, xs):
        def go(b, c):
            acc[:, :COLS] += dot(kv[0, b], xs[b, 0, :CH])
            acc[:, COLS:] += dot(kv[2, b], xs[b, 3, :CH])
            return c

        lax.fori_loop(0, 3, go, 0)

    conv_inner(zc, xcs)

    for b in range(3):
        n = BLOCKS[b] * 32
        rho = lax.broadcasted_iota(jnp.int32, (n, CH), 0)
        col = lax.broadcasted_iota(jnp.int32, (n, CH), 1)
        part = ((rho >> 3) & 3) * 4 + (rho & 3)
        src = 30 * (FIRST[b] + (rho >> 5)) + 15 * ((rho >> 2) & 1) + part - CH * b
        selm[b, :n, :] = jnp.where((part < 15) & (src == col), 1.0, 0.0).astype(bf16)

    def halo_wait(raw, up, down):
        @pl.when(has_prev)
        def _():
            up.wait_recv()

        @pl.when(jnp.logical_not(has_prev))
        def _():
            raw[0] = jnp.zeros((CH, COLS), bf16)

        @pl.when(has_next)
        def _():
            down.wait_recv()

        @pl.when(jnp.logical_not(has_next))
        def _():
            raw[3] = jnp.zeros((CH, COLS), bf16)

    halo_wait(xcr, halos[0], halos[1])

    @pl.when(has_next)
    def _():
        halos[2].start()

    @pl.when(has_prev)
    def _():
        halos[3].start()

    put_shifts(xcs, 0, xcr[0], xhi)
    put_shifts(xcs, 3, xcr[3], xhi)
    conv_outer(zc, xcs)

    def tile_of(cols4):
        q = lane >> 5
        picked = jnp.zeros((CH, COLS), f32)
        for i, v in enumerate(cols4):
            picked = jnp.where(q == i, v, picked)
        return jnp.sum(picked * emask[...], axis=0, keepdims=True)

    def a_copy(buf, send, recv, i, slot, t):
        return pltpu.make_async_remote_copy(
            src_ref=buf.at[slot],
            dst_ref=buf.at[slot],
            send_sem=send.at[i],
            recv_sem=recv.at[slot],
            device_id={"zl": t // NC, "core": t % NC},
            device_id_type=pl.DeviceIdType.MESH,
        )

    def b_copy(buf, send, recv, i, slot, t):
        return pltpu.make_async_remote_copy(
            src_ref=buf.at[slot],
            dst_ref=buf.at[slot],
            send_sem=send.at[i],
            recv_sem=recv.at[slot],
            device_id={"y": t},
            device_id_type=pl.DeviceIdType.MESH,
        )

    def start_all(copy, buf, send, recv, me, n, tile):
        buf[me] = tile

        def go(i, c):
            copy(buf, send, recv, i, me, (me + i) % n).start()
            return c

        lax.fori_loop(1, n, go, 0)

    def wait_all(copy, buf, send, recv, me, n):
        def go(i, c):
            t = (me + i) % n
            copy(buf, send, recv, i, t, t).wait_recv()
            return c

        lax.fori_loop(1, n, go, 0)
        return jnp.sum(buf[...], axis=0)

    def sent_all(copy, buf, send, recv, me, n):
        def go(i, c):
            copy(buf, send, recv, i, me, (me + i) % n).wait_send()
            return c

        lax.fori_loop(1, n, go, 0)

    z = zc[...]
    start_all(
        a_copy, ra, as_, ar, m, NM,
        tile_of((jnp.sum(z, axis=1, keepdims=True), jnp.sum(z * z, axis=1, keepdims=True))),
    )

    cp_xn.wait()
    put_shifts(xns, 1, xnr[1])
    put_shifts(xns, 2, xnr[2])
    conv_inner(zn, xns)
    start_all(b_copy, rb, bs, br, yy, NY, wait_all(a_copy, ra, as_, ar, m, NM))
    halo_wait(xnr, halos[2], halos[3])
    put_shifts(xns, 0, xnr[0])
    put_shifts(xns, 3, xnr[3])
    conv_outer(zn, xns)
    zv = zn[...]
    next_sums = (jnp.sum(zv, axis=1, keepdims=True), jnp.sum(zv * zv, axis=1, keepdims=True))
    cp_go.wait()
    total = wait_all(b_copy, rb, bs, br, yy, NY)

    def column(row, block):
        keep = (lane >> 5) == block
        return jnp.sum(jnp.where(keep, emask[...] * row, 0.0), axis=1, keepdims=True)

    def moments(tile, first):
        row = tile / COUNT
        mean_row = pltpu.roll(jnp.broadcast_to(row, (8, COLS)), (128 - 32 * first) % 128, 1)[:1]
        square_row = pltpu.roll(jnp.broadcast_to(row, (8, COLS)), (128 - 32 * (first + 1)) % 128, 1)[:1]
        rstd_row = lax.rsqrt(square_row - mean_row * mean_row + EPS)
        return column(mean_row, 0), column(rstd_row, 0)

    mean_c, rstd_c = moments(total, 0)
    normed = (zc[...] - mean_c) * rstd_c
    nrm[...] = normed
    affine = normed * gam[...] + bet[...]
    sig = jax.nn.sigmoid(affine)
    grad = jnp.concatenate([gor[0], gor[1]], axis=1).astype(f32)
    grad_n = grad * (sig * (1.0 + affine * (1.0 - sig))) * gam[...]
    gn[...] = grad_n
    start_all(
        a_copy, ra2, as2, ar2, m, NM,
        tile_of(
            (
                jnp.sum(grad_n, axis=1, keepdims=True),
                jnp.sum(grad_n * normed, axis=1, keepdims=True),
            )
            + next_sums
        ),
    )
    start_all(b_copy, rb2, bs2, br2, yy, NY, wait_all(a_copy, ra2, as2, ar2, m, NM))
    total2 = wait_all(b_copy, rb2, bs2, br2, yy, NY)
    row2 = total2 / COUNT
    mean_1, mean_2 = column(row2, 0), column(row2, 1)
    gz = (rstd_c * (gn[...] - mean_1 - nrm[...] * mean_2)).astype(bf16)
    gzo[0] = gz[:, :COLS]
    gzo[1] = gz[:, COLS:]

    def gz_copy(to_next):
        return pltpu.make_async_remote_copy(
            src_ref=gzo.at[1] if to_next else gzo.at[0],
            dst_ref=gzh.at[0] if to_next else gzh.at[1],
            send_sem=ghs.at[0 if to_next else 1],
            recv_sem=ghr.at[0 if to_next else 1],
            device_id=next_id if to_next else prev_id,
            device_id_type=pl.DeviceIdType.MESH,
        )

    gz_next, gz_prev = gz_copy(True), gz_copy(False)

    @pl.when(has_next)
    def _():
        gz_next.start()

    @pl.when(has_prev)
    def _():
        gz_prev.start()

    picked = [dot(selm[b, : BLOCKS[b] * 32], gz).astype(bf16) for b in range(3)]

    def put(ref, rows, piece, add):
        if add:
            ref[rows, :] += piece
        else:
            ref[rows, :] = piece

    def blocks(a, b):
        for d in range(BLOCKS[b]):
            block = 32 * a + FIRST[b] + d
            yield d, block // NM, gacc.at[(block // 2) % NZL, block % 2], d == 0 and b > 0

    for a in range(3):
        for b in range(3):
            out = dot(picked[b], jnp.concatenate([xcs[b, a, :MAIN], xcs[b, a + 1, :MAIN]], axis=1), NT)
            for d, row, ref, again in blocks(a, b):
                for u in range(NX):
                    top = d * 32 + u * 8
                    put(ref.at[u], slice(row * 8, row * 8 + 8), out[top : top + 8, :LANES], again)
                    put(ref.at[u], slice(64 + row * 8, 72 + row * 8), out[top : top + 8, LANES:], again)

    def rest_gradient():
        for a in range(3):
            for b in range(3):
                low = min(max(NH // 2 - 32 * a - FIRST[b], 0), BLOCKS[b])
                rest = []
                if low > 0:
                    source = jnp.concatenate([xcs[b, a, MAIN:], xcs[b, a + 1, MAIN:]], axis=1)
                    rest.append(dot(picked[b][: low * 32], source, NT))
                if low < BLOCKS[b]:
                    source = jnp.concatenate([xhi[b, a], xhi[b, a + 1]], axis=1)
                    rest.append(dot(picked[b][low * 32 :], source, NT))
                for d, row, ref, again in blocks(a, b):
                    part, at = (rest[0], d) if d < low else (rest[-1], d - low)
                    for u in range(NX):
                        top = at * 32 + u * 8
                        at_row = 128 + row % 4 * 8
                        put(ref.at[u], slice(at_row, at_row + 8), part[top : top + 8], again or row >= 4)

    PARTS = (pl.ds(0, 128), pl.ds(128, 32))

    def send_core(k, part):
        rows = PARTS[part]
        return pltpu.make_async_remote_copy(
            src_ref=s1.at[k, :, rows], dst_ref=r1.at[k, :, rows],
            send_sem=c1s.at[part, k], recv_sem=c1r.at[part, k],
            device_id={"core": 1 - co}, device_id_type=pl.DeviceIdType.MESH,
        )

    pair = xx + 1 - 2 * (xx % 2)
    mirror = 3 - xx

    def partners(k):
        return (pair, mirror) if k < 3 else (mirror, pair)

    def second_of_first(k):
        first = partners(k)[0]
        return 3 - first if k < 3 else first + 1 - 2 * (first % 2)

    def send_x1(k, part):
        rows = PARTS[part]
        return pltpu.make_async_remote_copy(
            src_ref=s2.at[k, :, rows], dst_ref=r2.at[k, :, rows],
            send_sem=c2s.at[part, k], recv_sem=c2r.at[part, k],
            device_id={"x": partners(k)[0]}, device_id_type=pl.DeviceIdType.MESH,
        )

    def send_x2(k):
        return pltpu.make_async_remote_copy(
            src_ref=s3.at[k], dst_ref=r3.at[k], send_sem=c3s.at[k], recv_sem=c3r.at[k],
            device_id={"x": partners(k)[1]}, device_id_type=pl.DeviceIdType.MESH,
        )

    def y_copy(k, i, slot, src, t):
        return pltpu.make_async_remote_copy(
            src_ref=s4.at[k, src], dst_ref=r4.at[k, slot], send_sem=c4s.at[k, i],
            recv_sem=c4r.at[k, slot], device_id={"y": t}, device_id_type=pl.DeviceIdType.MESH,
        )

    def z_copy(k, h, slot):
        return pltpu.make_async_remote_copy(
            src_ref=s5.at[k], dst_ref=r5.at[slot], send_sem=c5s.at[k, h], recv_sem=c5r.at[slot],
            device_id={"zl": k, "zh": h}, device_id_type=pl.DeviceIdType.MESH,
        )

    def z_first(k, h, slot):
        return pltpu.make_async_remote_copy(
            src_ref=s7.at[k, h], dst_ref=r7.at[slot], send_sem=c7s.at[k, h], recv_sem=c7r.at[slot],
            device_id={"zl": k, "zh": h}, device_id_type=pl.DeviceIdType.MESH,
        )

    def y_second(i, slot, t):
        return pltpu.make_async_remote_copy(
            src_ref=s8.at[t // 2], dst_ref=r8.at[slot], send_sem=c8s.at[i], recv_sem=c8r.at[slot],
            device_id={"y": t}, device_id_type=pl.DeviceIdType.MESH,
        )

    forward = pltpu.make_async_remote_copy(
        src_ref=mine, dst_ref=before, send_sem=fsem.at[0], recv_sem=fsem.at[1],
        device_id={"x": jnp.minimum(xx + 1, NX - 1)}, device_id_type=pl.DeviceIdType.MESH,
    )

    def summed(k, u):
        return gacc[k, co, u] + r1[k, u].astype(f32)

    def step_core(k, part):
        rows = PARTS[part]
        s1[k, :, rows, :] = gacc[k, 1 - co, :, rows, :].astype(bf16)
        send_core(k, part).start()

    def step_x1(k, part):
        send_core(k, part).wait_recv()
        rows = PARTS[part]
        for i, u in enumerate((partners(k)[0], second_of_first(k))):
            s2[k, i, rows, :] = (gacc[k, co, u, rows, :] + r1[k, u, rows, :].astype(f32)).astype(bf16)
        send_x1(k, part).start()

    def step_x2(k):
        send_x1(k, 0).wait_recv()
        send_x1(k, 1).wait_recv()
        s3[k] = (summed(k, partners(k)[1]) + r2[k, 1].astype(f32)).astype(bf16)
        send_x2(k).start()

    def step_y(k):
        send_x2(k).wait_recv()
        val = summed(k, xx) + r2[k, 0].astype(f32) + r3[k].astype(f32)
        bown[k, :, :8, :] = val[:64].reshape(NY, 8, LANES)
        rest = val[128:].reshape(NY // 2, 8, LANES)
        bown[k, : NY // 2, 8:, :] = rest
        bown[k, NY // 2 :, 8:, :] = rest
        s4[k] = bown[k].astype(bf16)
        for t in range(NY):
            for h in range(NZH):
                top = 64 + t * 8 + h * 4
                zown[k, h, t * 4 : t * 4 + 4, :] = val[top : top + 4]
        s7[k] = zown[k].astype(bf16)

        def go(i, c):
            t = (yy + i) % NY
            y_copy(k, i, yy, t, t).start()
            return c

        lax.fori_loop(1, NY, go, 0)
        for h in range(NZH):

            @pl.when(jnp.logical_or(zl != k, zh != h))
            def _():
                z_first(k, h, z12).start()

    def middle():
        def take(i, acc):
            t = (z12 + i) % NZ
            z_first(0, 0, t).wait_recv()
            return acc + r7[t].astype(f32)

        val = lax.fori_loop(1, NZ, take, zown[zl, zh]).reshape(NY // 2, 8, LANES)
        mid[...] = val
        s8[...] = val.astype(bf16)

        def go(i, c):
            t = (yy + i) % NY
            y_second(i, yy, t).start()
            return c

        lax.fori_loop(1, NY, go, 0)

    def middle_end():
        def go(i, acc):
            t = (yy + i) % NY
            y_second(i, t, t).wait_recv()
            return acc + r8[t].astype(f32)

        return lax.fori_loop(1, NY, go, mid[yy // 2])

    def step_z(k):
        def go(i, acc):
            t = (yy + i) % NY
            y_copy(k, i, t, t, t).wait_recv()
            return acc + r4[k, t].astype(f32)

        val = lax.fori_loop(1, NY, go, bown[k, yy])
        cown[k] = val
        s5[k] = val.astype(bf16)
        for h in range(NZH):
            @pl.when(jnp.logical_or(zl != k, zh != h))
            def _():
                z_copy(k, h, z12).start()

    for k in ORDER:
        step_core(k, 0)
    for k in ORDER:
        step_x1(k, 0)
    rest_gradient()
    for k in ORDER:
        step_core(k, 1)
    for k in ORDER:
        step_x1(k, 1)

    for step in range(len(ORDER) + 2):
        if step < 6:
            step_x2(ORDER[step])
        if step >= 2:
            step_y(ORDER[step - 2])
    for k in ORDER:
        step_z(k)
    middle()

    mean_n = column(row2, 2)
    square_n = column(row2, 3)
    rstd_n = lax.rsqrt(square_n - mean_n * mean_n + EPS)
    affine_n = (zn[...] - mean_n) * rstd_n * gam[...] + bet[...]
    y_next = (affine_n * jax.nn.sigmoid(affine_n)).astype(bf16)
    y_out[0, 0] = y_next[:, :COLS]
    y_out[0, 1] = y_next[:, COLS:]

    @pl.when(has_prev)
    def _():
        gz_next.wait_recv()

    @pl.when(jnp.logical_not(has_prev))
    def _():
        gzh[0] = jnp.zeros((CH, COLS), bf16)

    @pl.when(has_next)
    def _():
        gz_prev.wait_recv()

    @pl.when(jnp.logical_not(has_next))
    def _():
        gzh[1] = jnp.zeros((CH, COLS), bf16)

    put_shifts(gzs, 0, gzh[0])
    put_shifts(gzs, 1, gzo[0])
    put_shifts(gzs, 2, gzo[1])
    put_shifts(gzs, 3, gzh[1])
    zc[...] = jnp.zeros_like(zc)

    def back(t, c):
        a, b = t // 3, t % 3
        source = jnp.concatenate([gzs[2 - b, 2 - a, :CH], gzs[2 - b, 3 - a, :CH]], axis=1)
        zc[...] += dot(kv[a, b], source, TN)
        return c

    lax.fori_loop(0, 9, back, 0)
    grad_x = zc[...].astype(bf16)
    gx_out[0, 0] = grad_x[:, :COLS]
    gx_out[0, 1] = grad_x[:, COLS:]

    def gather_z(i, acc):
        t = (z12 + i) % NZ
        z_copy(0, 0, t).wait_recv()
        return acc + r5[t].astype(f32)

    total_z = lax.fori_loop(1, NZ, gather_z, cown[zl])
    mine[:8] = total_z[:8]
    mine[8:16] = middle_end()
    mine[16:] = total_z[8:]

    @pl.when(xx < NX - 1)
    def _():
        forward.start()

    @pl.when(has_next)
    def _():
        halos[0].wait_send()
        halos[2].wait_send()
        gz_next.wait_send()

    @pl.when(has_prev)
    def _():
        halos[1].wait_send()
        halos[3].wait_send()
        gz_prev.wait_send()

    sent_all(a_copy, ra, as_, ar, m, NM)
    sent_all(b_copy, rb, bs, br, yy, NY)
    sent_all(a_copy, ra2, as2, ar2, m, NM)
    sent_all(b_copy, rb2, bs2, br2, yy, NY)
    for k in range(NZL):
        for part in range(2):
            send_core(k, part).wait_send()
            send_x1(k, part).wait_send()
        send_x2(k).wait_send()

        def sent_y(i, c):
            y_copy(k, i, yy, (yy + i) % NY, (yy + i) % NY).wait_send()
            return c

        lax.fori_loop(1, NY, sent_y, 0)
        for h in range(NZH):
            @pl.when(jnp.logical_or(zl != k, zh != h))
            def _():
                z_copy(k, h, z12).wait_send()
                z_first(k, h, z12).wait_send()

    def sent_second(i, c):
        y_second(i, yy, (yy + i) % NY).wait_send()
        return c

    lax.fori_loop(1, NY, sent_second, 0)
    gk_out[0] = mine[...]

    @pl.when(xx > 0)
    def _():
        forward.wait_recv()

    @pl.when(xx == 0)
    def _():
        before[...] = jnp.zeros_like(before)

    gk_out[1] = before[...]

    @pl.when(xx < NX - 1)
    def _():
        forward.wait_send()


def last(y_in, gx_in, raw, y_out, gx_out, gk_out, rows, sem):
    back = [
        pltpu.make_async_copy(y_in, y_out, sem.at[0]),
        pltpu.make_async_copy(gx_in, gx_out, sem.at[1]),
    ]
    for cp in back:
        cp.start()
    second, high = lax.axis_index("zh") == 1, lax.axis_index("y") >= NY // 2
    odd = lax.axis_index("y") % 2 == 1
    for i in range(2):
        tile = raw[i]
        rest = tile[16:]
        parts = (tile[:8], tile[8:16], jnp.where(high, pltpu.roll(rest, REST, 1), rest))
        for t, p in enumerate(parts):
            four = jnp.where(odd if t == 1 else second, p[4:], p[:4])
            lanes = slice(t * LANES, (t + 1) * LANES)
            if i == 0:
                rows[1:5, lanes] = four
            else:
                rows[0:1, lanes] = four[3:]
    share = 9 * CH * CH // (NH * NZH * NX)
    for v in range(NX):

        @pl.when(lax.axis_index("x") == v)
        def _():
            for start in range(0, share, LANES):
                n = min(LANES, share - start)
                r, col = divmod(share * v + start, CH)
                r = r - 4 * v + 1
                k = min(n, CH - col)
                piece = rows[r : r + 1, col : col + k]
                if k < n:
                    piece = jnp.concatenate([piece, rows[r + 1 : r + 2, : n - k]], axis=1)
                gk_out[pl.ds(start, n)] = piece.reshape(n)

    for cp in back:
        cp.wait()


def local(x_next, x_cur, grad_out, kernel, gamma, beta):
    vmem = pl.BlockSpec(memory_space=pltpu.VMEM)
    hbm = pl.BlockSpec(memory_space=pltpu.HBM)
    dma = pltpu.SemaphoreType.DMA
    V = pltpu.VMEM
    scratch = [
        V((CH,), f32), V((CH,), f32),
        V((4, CH, COLS), bf16), V((4, CH, COLS), bf16), V((2, CH, COLS), bf16),
        V((3, 3, CH, CH), bf16),
        V((3, 4, CH + REST, COLS), bf16), V((3, 4, 2 * REST, COLS), bf16), V((3, 4, CH, COLS), bf16),
        V((2, CH, COLS), bf16), V((2, CH, COLS), bf16), V((3, 4, CH, COLS), bf16),
        V((CH, 2 * COLS), f32), V((CH, 2 * COLS), f32), V((CH, 2 * COLS), f32), V((CH, 2 * COLS), f32),
        V((CH, COLS), f32), V((CH, 1), f32), V((CH, 1), f32),
        V((3, 32 * max(BLOCKS), CH), bf16),
        V((NM, 1, COLS), f32), V((NY, 1, COLS), f32), V((NM, 1, COLS), f32), V((NY, 1, COLS), f32),
        V((NZL, NC, NX, TALL, LANES), f32),
        V((NZL, NX, TALL, LANES), bf16), V((NZL, NX, TALL, LANES), bf16),
        V((NZL, 2, TALL, LANES), bf16), V((NZL, 2, TALL, LANES), bf16),
        V((NZL, TALL, LANES), bf16), V((NZL, TALL, LANES), bf16),
        V((NZL, NY, 16, LANES), bf16), V((NZL, NY, 16, LANES), bf16),
        V((NZL, NY, 16, LANES), f32),
        V((NZL, 16, LANES), bf16), V((NZL, 16, LANES), f32),
        V((NZ, 16, LANES), bf16),
        V((NZL, NZH, NY * 4, LANES), f32), V((NZL, NZH, NY * 4, LANES), bf16), V((NZ, NY * 4, LANES), bf16),
        V((NY // 2, 8, LANES), f32), V((NY // 2, 8, LANES), bf16), V((NY, 8, LANES), bf16),
        V((24, LANES), f32), V((24, LANES), f32),
        dma((6,)), dma((4,)), dma((4,)), dma((2,)), dma((2,)),
        dma((NM,)), dma((NM,)), dma((NY,)), dma((NY,)),
        dma((NM,)), dma((NM,)), dma((NY,)), dma((NY,)),
        dma((2, NZL)), dma((2, NZL)), dma((2, NZL)), dma((2, NZL)), dma((NZL,)), dma((NZL,)),
        dma((NZL, NY)), dma((NZL, NY)), dma((NZL, NZH)), dma((NZ,)),
        dma((NZL, NZH)), dma((NZ,)), dma((NY,)), dma((NY,)), dma((2,)),
    ]
    y_next, grad_x, quarters = pl.pallas_call(
        body,
        out_shape=(
            pltpu.VMEM(x_next.shape, bf16),
            pltpu.VMEM(x_next.shape, bf16),
            pltpu.VMEM((2, 24, LANES), f32),
        ),
        in_specs=[hbm] * 6,
        out_specs=(vmem, vmem, vmem),
        scratch_shapes=scratch,
        compiler_params=pltpu.CompilerParams(
            collective_id=0, has_side_effects=True, vmem_limit_bytes=40 * 1024 * 1024
        ),
    )(*(pltpu.with_memory_space_constraint(v, pltpu.HBM) for v in (x_next, x_cur, grad_out, kernel, gamma, beta)))
    return pl.pallas_call(
        last,
        out_shape=(
            jax.ShapeDtypeStruct(x_next.shape, bf16),
            jax.ShapeDtypeStruct(x_next.shape, bf16),
            jax.ShapeDtypeStruct((9 * CH * CH // (NH * NZH * NX),), f32),
        ),
        in_specs=[vmem, vmem, vmem],
        out_specs=(hbm, hbm, vmem),
        scratch_shapes=[V((8, 3 * LANES), f32), dma((2,))],
        compiler_params=pltpu.CompilerParams(vmem_limit_bytes=8 * 1024 * 1024),
    )(y_next, grad_x, quarters)


def solution(mesh):
    torus = Mesh(mesh.devices.reshape(NY, NZL, NC, NZH, NX), HEIGHT + DP)
    image = P(DP, HEIGHT, None, None)
    return jax.shard_map(
        local,
        mesh=torus,
        in_specs=(image, image, image, P(), P(), P()),
        out_specs=(image, image, P(HEIGHT + DP)),
        check_vma=False,
    )
```

```python
import jax
import jax.numpy as jnp
from jax import lax
from jax.experimental import pallas as pl
from jax.experimental.pallas import tpu as pltpu
from jax.sharding import Mesh
from jax.sharding import PartitionSpec as P

CH = 320
COLS = 128
LANES = 128
MAIN = 256
REST = CH - MAIN
TALL = 160
GROUP = 10
NY, NZL, NC, NZH, NX = 8, 6, 2, 2, 4
NM = NZL * NC
NH = NY * NM
NZ = NZL * NZH
COUNT = 192 * GROUP * COLS
EPS = 1e-05
HEIGHT = ("y", "zl", "core")
DP = ("zh", "x")
FIRST = (0, 10, 21)
BLOCKS = (11, 12, 11)
ORDER = (0, 3, 1, 4, 2, 5)

f32 = jnp.float32
bf16 = jnp.bfloat16


def dot(a, b, dims=(((1,), (0,)), ((), ()))):
    return lax.dot_general(a, b, dims, preferred_element_type=f32)


NT = (((1,), (1,)), ((), ()))
TN = (((0,), (0,)), ((), ()))


def body(
    xn_in, xc_in, go_in, k_in, gam_in, bet_in,
    y_out, gx_out, gk_out,
    gam_row, bet_row, xcr, xnr, gor, kv, xcs, xhi, xns, gzo, gzh, gzs,
    zc, zn, nrm, gn, emask, gam, bet, selm,
    ra, rb, ra2, rb2,
    gacc, s1, r1, s2, r2, s3, r3, s4, r4, bown, s5, cown, r5, zown, s7, r7, mid, s8, r8, mine, before,
    lsem, hs, hr, ghs, ghr, as_, ar, bs, br, as2, ar2, bs2, br2,
    c1s, c1r, c2s, c2r, c3s, c3r, c4s, c4r, c5s, c5r, c7s, c7r, c8s, c8r, fsem,
):
    yy, zl, co = lax.axis_index("y"), lax.axis_index("zl"), lax.axis_index("core")
    zh, xx = lax.axis_index("zh"), lax.axis_index("x")
    m = zl * NC + co
    pos = yy * NM + m
    z12 = zl * NZH + zh

    def height_id(p):
        return {"y": p // NM, "zl": (p // NC) % NZL, "core": p % NC}

    has_prev, has_next = pos > 0, pos < NH - 1
    prev_id, next_id = height_id(jnp.maximum(pos - 1, 0)), height_id(jnp.minimum(pos + 1, NH - 1))

    barrier = pltpu.get_barrier_semaphore()

    def greet(device_id):
        pl.semaphore_signal(barrier, inc=1, device_id=device_id, device_id_type=pl.DeviceIdType.MESH)

    @pl.when(has_prev)
    def _():
        greet(prev_id)

    @pl.when(has_next)
    def _():
        greet(next_id)

    def far_z(i, c):
        greet({"zl": i, "zh": 1 - zh})
        return c

    lax.fori_loop(0, NZL, far_z, 0, unroll=True)

    def far_m(i, c):
        t = (m + i) % NM
        greet({"zl": t // NC, "core": t % NC})
        return c

    lax.fori_loop(1, NM, far_m, 0, unroll=True)

    def far_y(i, c):
        greet({"y": (yy + i) % NY})
        return c

    lax.fori_loop(1, NY, far_y, 0, unroll=True)

    def far_x(i, c):
        greet({"x": (xx + i) % NX})
        return c

    lax.fori_loop(1, NX, far_x, 0, unroll=True)

    cp_xc = pltpu.make_async_copy(xc_in.at[0], xcr.at[pl.ds(1, 2)], lsem.at[0])
    cp_k = pltpu.make_async_copy(k_in, kv, lsem.at[1])
    cp_xn = pltpu.make_async_copy(xn_in.at[0], xnr.at[pl.ds(1, 2)], lsem.at[2])
    cp_go = pltpu.make_async_copy(go_in.at[0], gor, lsem.at[3])
    cp_gam = pltpu.make_async_copy(gam_in, gam_row, lsem.at[4])
    cp_bet = pltpu.make_async_copy(bet_in, bet_row, lsem.at[5])
    for cp in (cp_xc, cp_gam, cp_bet, cp_k, cp_xn, cp_go):
        cp.start()

    greeted = NZL + (NM - 1) + (NY - 1) + (NX - 1)
    pl.semaphore_wait(barrier, greeted + has_prev.astype(jnp.int32) + has_next.astype(jnp.int32))

    def halo(src, dst, to_next, i, send, recv):
        return pltpu.make_async_remote_copy(
            src_ref=src.at[0, 1] if to_next else src.at[0, 0],
            dst_ref=dst.at[0] if to_next else dst.at[3],
            send_sem=send.at[i],
            recv_sem=recv.at[i],
            device_id=next_id if to_next else prev_id,
            device_id_type=pl.DeviceIdType.MESH,
        )

    halos = (
        halo(xc_in, xcr, True, 0, hs, hr),
        halo(xc_in, xcr, False, 1, hs, hr),
        halo(xn_in, xnr, True, 2, hs, hr),
        halo(xn_in, xnr, False, 3, hs, hr),
    )

    @pl.when(has_next)
    def _():
        halos[0].start()

    @pl.when(has_prev)
    def _():
        halos[1].start()

    rows_i = lax.broadcasted_iota(jnp.int32, (CH, COLS), 0)
    lane_i = lax.broadcasted_iota(jnp.int32, (CH, COLS), 1)
    rel = rows_i - GROUP * (lane_i & 31)
    emask[...] = jnp.where((rel >= 0) & (rel < GROUP), 1.0, 0.0).astype(f32)
    eye = lax.broadcasted_iota(jnp.int32, (CH, CH), 0) == lax.broadcasted_iota(jnp.int32, (CH, CH), 1)
    cp_gam.wait()
    cp_bet.wait()
    gam[...] = jnp.sum(jnp.where(eye, gam_row[...].reshape(1, CH), 0.0), axis=1, keepdims=True)
    bet[...] = jnp.sum(jnp.where(eye, bet_row[...].reshape(1, CH), 0.0), axis=1, keepdims=True)
    zc[...] = jnp.zeros_like(zc)
    zn[...] = jnp.zeros_like(zn)
    for b in range(3):
        for r in range(4):
            xcs[b, r, CH:, :] = jnp.zeros((REST, COLS), bf16)
            xhi[b, r, :REST, :] = jnp.zeros((REST, COLS), bf16)

    lane = lax.broadcasted_iota(jnp.int32, (CH, COLS), 1)

    def put_shifts(dst, row, v, high=None):
        wide = v.astype(f32)
        moved = (
            jnp.where(lane == 0, 0.0, pltpu.roll(wide, 1, 1)).astype(bf16),
            v,
            jnp.where(lane == COLS - 1, 0.0, pltpu.roll(wide, COLS - 1, 1)).astype(bf16),
        )
        for b in range(3):
            dst[b, row, :CH, :] = moved[b]
            if high is not None:
                high[b, row, REST:, :] = moved[b][MAIN:]

    cp_xc.wait()
    put_shifts(xcs, 1, xcr[1], xhi)
    put_shifts(xcs, 2, xcr[2], xhi)

    cp_k.wait()

    def conv_inner(acc, xs):
        def go(b, c):
            x1, x2 = xs[b, 1, :CH], xs[b, 2, :CH]
            acc[...] += dot(kv[1, b], jnp.concatenate([x1, x2], axis=1))
            acc[:, COLS:] += dot(kv[0, b], x1)
            acc[:, :COLS] += dot(kv[2, b], x2)
            return c

        lax.fori_loop(0, 3, go, 0)

    def conv_outer(acc, xs):
        def go(b, c):
            acc[:, :COLS] += dot(kv[0, b], xs[b, 0, :CH])
            acc[:, COLS:] += dot(kv[2, b], xs[b, 3, :CH])
            return c

        lax.fori_loop(0, 3, go, 0)

    conv_inner(zc, xcs)

    for b in range(3):
        n = BLOCKS[b] * 32
        rho = lax.broadcasted_iota(jnp.int32, (n, CH), 0)
        col = lax.broadcasted_iota(jnp.int32, (n, CH), 1)
        part = ((rho >> 3) & 3) * 4 + (rho & 3)
        src = 30 * (FIRST[b] + (rho >> 5)) + 15 * ((rho >> 2) & 1) + part - CH * b
        selm[b, :n, :] = jnp.where((part < 15) & (src == col), 1.0, 0.0).astype(bf16)

    def halo_wait(raw, up, down):
        @pl.when(has_prev)
        def _():
            up.wait_recv()

        @pl.when(jnp.logical_not(has_prev))
        def _():
            raw[0] = jnp.zeros((CH, COLS), bf16)

        @pl.when(has_next)
        def _():
            down.wait_recv()

        @pl.when(jnp.logical_not(has_next))
        def _():
            raw[3] = jnp.zeros((CH, COLS), bf16)

    halo_wait(xcr, halos[0], halos[1])

    @pl.when(has_next)
    def _():
        halos[2].start()

    @pl.when(has_prev)
    def _():
        halos[3].start()

    put_shifts(xcs, 0, xcr[0], xhi)
    put_shifts(xcs, 3, xcr[3], xhi)
    conv_outer(zc, xcs)

    def tile_of(cols4):
        q = lane >> 5
        picked = jnp.zeros((CH, COLS), f32)
        for i, v in enumerate(cols4):
            picked = jnp.where(q == i, v, picked)
        return jnp.sum(picked * emask[...], axis=0, keepdims=True)

    def a_copy(buf, send, recv, i, slot, t):
        return pltpu.make_async_remote_copy(
            src_ref=buf.at[slot],
            dst_ref=buf.at[slot],
            send_sem=send.at[i],
            recv_sem=recv.at[slot],
            device_id={"zl": t // NC, "core": t % NC},
            device_id_type=pl.DeviceIdType.MESH,
        )

    def b_copy(buf, send, recv, i, slot, t):
        return pltpu.make_async_remote_copy(
            src_ref=buf.at[slot],
            dst_ref=buf.at[slot],
            send_sem=send.at[i],
            recv_sem=recv.at[slot],
            device_id={"y": t},
            device_id_type=pl.DeviceIdType.MESH,
        )

    def start_all(copy, buf, send, recv, me, n, tile):
        buf[me] = tile

        def go(i, c):
            copy(buf, send, recv, i, me, (me + i) % n).start()
            return c

        lax.fori_loop(1, n, go, 0, unroll=True)

    def wait_all(copy, buf, send, recv, me, n):
        def go(i, c):
            t = (me + i) % n
            copy(buf, send, recv, i, t, t).wait_recv()
            return c

        lax.fori_loop(1, n, go, 0, unroll=True)
        return jnp.sum(buf[...], axis=0)

    def sent_all(copy, buf, send, recv, me, n):
        def go(i, c):
            copy(buf, send, recv, i, me, (me + i) % n).wait_send()
            return c

        lax.fori_loop(1, n, go, 0)

    z = zc[...]
    start_all(
        a_copy, ra, as_, ar, m, NM,
        tile_of((jnp.sum(z, axis=1, keepdims=True), jnp.sum(z * z, axis=1, keepdims=True))),
    )

    cp_xn.wait()
    put_shifts(xns, 1, xnr[1])
    put_shifts(xns, 2, xnr[2])
    conv_inner(zn, xns)
    start_all(b_copy, rb, bs, br, yy, NY, wait_all(a_copy, ra, as_, ar, m, NM))
    halo_wait(xnr, halos[2], halos[3])
    put_shifts(xns, 0, xnr[0])
    put_shifts(xns, 3, xnr[3])
    conv_outer(zn, xns)
    zv = zn[...]
    next_sums = (jnp.sum(zv, axis=1, keepdims=True), jnp.sum(zv * zv, axis=1, keepdims=True))
    cp_go.wait()
    total = wait_all(b_copy, rb, bs, br, yy, NY)

    def column(row, block):
        keep = (lane >> 5) == block
        return jnp.sum(jnp.where(keep, emask[...] * row, 0.0), axis=1, keepdims=True)

    def moments(tile, first):
        row = tile / COUNT
        mean_row = pltpu.roll(jnp.broadcast_to(row, (8, COLS)), (128 - 32 * first) % 128, 1)[:1]
        square_row = pltpu.roll(jnp.broadcast_to(row, (8, COLS)), (128 - 32 * (first + 1)) % 128, 1)[:1]
        rstd_row = lax.rsqrt(square_row - mean_row * mean_row + EPS)
        return column(mean_row, 0), column(rstd_row, 0)

    mean_c, rstd_c = moments(total, 0)
    normed = (zc[...] - mean_c) * rstd_c
    nrm[...] = normed
    affine = normed * gam[...] + bet[...]
    sig = jax.nn.sigmoid(affine)
    grad = jnp.concatenate([gor[0], gor[1]], axis=1).astype(f32)
    grad_n = grad * (sig * (1.0 + affine * (1.0 - sig))) * gam[...]
    gn[...] = grad_n
    start_all(
        a_copy, ra2, as2, ar2, m, NM,
        tile_of(
            (
                jnp.sum(grad_n, axis=1, keepdims=True),
                jnp.sum(grad_n * normed, axis=1, keepdims=True),
            )
            + next_sums
        ),
    )
    start_all(b_copy, rb2, bs2, br2, yy, NY, wait_all(a_copy, ra2, as2, ar2, m, NM))
    total2 = wait_all(b_copy, rb2, bs2, br2, yy, NY)
    row2 = total2 / COUNT
    mean_1, mean_2 = column(row2, 0), column(row2, 1)
    gz = (rstd_c * (gn[...] - mean_1 - nrm[...] * mean_2)).astype(bf16)
    gzo[0] = gz[:, :COLS]
    gzo[1] = gz[:, COLS:]

    def gz_copy(to_next):
        return pltpu.make_async_remote_copy(
            src_ref=gzo.at[1] if to_next else gzo.at[0],
            dst_ref=gzh.at[0] if to_next else gzh.at[1],
            send_sem=ghs.at[0 if to_next else 1],
            recv_sem=ghr.at[0 if to_next else 1],
            device_id=next_id if to_next else prev_id,
            device_id_type=pl.DeviceIdType.MESH,
        )

    gz_next, gz_prev = gz_copy(True), gz_copy(False)

    @pl.when(has_next)
    def _():
        gz_next.start()

    @pl.when(has_prev)
    def _():
        gz_prev.start()

    picked = [dot(selm[b, : BLOCKS[b] * 32], gz).astype(bf16) for b in range(3)]

    def put(ref, rows, piece, add):
        if add:
            ref[rows, :] += piece
        else:
            ref[rows, :] = piece

    for a in range(3):
        for b in range(3):
            first = 32 * a + FIRST[b]
            low = min(max(NH // 2 - first, 0), BLOCKS[b])
            out = dot(picked[b], jnp.concatenate([xcs[b, a, :MAIN], xcs[b, a + 1, :MAIN]], axis=1), NT)
            rest = []
            if low > 0:
                source = jnp.concatenate([xcs[b, a, MAIN:], xcs[b, a + 1, MAIN:]], axis=1)
                rest.append(dot(picked[b][: low * 32], source, NT))
            if low < BLOCKS[b]:
                source = jnp.concatenate([xhi[b, a], xhi[b, a + 1]], axis=1)
                rest.append(dot(picked[b][low * 32 :], source, NT))
            for d in range(BLOCKS[b]):
                block = first + d
                row = block // NM
                part, at = (rest[0], d) if d < low else (rest[-1], d - low)
                again = d == 0 and b > 0
                for u in range(NX):
                    ref = gacc.at[(block // 2) % NZL, block % 2, u]
                    top = d * 32 + u * 8
                    put(ref, slice(row * 8, row * 8 + 8), out[top : top + 8, :LANES], again)
                    put(ref, slice(64 + row * 8, 72 + row * 8), out[top : top + 8, LANES:], again)
                    top = at * 32 + u * 8
                    at_row = 128 + row % 4 * 8
                    put(ref, slice(at_row, at_row + 8), part[top : top + 8], again or row >= 4)

    def send_core(k):
        return pltpu.make_async_remote_copy(
            src_ref=s1.at[k], dst_ref=r1.at[k], send_sem=c1s.at[k], recv_sem=c1r.at[k],
            device_id={"core": 1 - co}, device_id_type=pl.DeviceIdType.MESH,
        )

    pair = xx + 1 - 2 * (xx % 2)
    mirror = 3 - xx

    def partners(k):
        return (pair, mirror) if k < 3 else (mirror, pair)

    def second_of_first(k):
        first = partners(k)[0]
        return 3 - first if k < 3 else first + 1 - 2 * (first % 2)

    def send_x1(k):
        return pltpu.make_async_remote_copy(
            src_ref=s2.at[k], dst_ref=r2.at[k], send_sem=c2s.at[k], recv_sem=c2r.at[k],
            device_id={"x": partners(k)[0]}, device_id_type=pl.DeviceIdType.MESH,
        )

    def send_x2(k):
        return pltpu.make_async_remote_copy(
            src_ref=s3.at[k], dst_ref=r3.at[k], send_sem=c3s.at[k], recv_sem=c3r.at[k],
            device_id={"x": partners(k)[1]}, device_id_type=pl.DeviceIdType.MESH,
        )

    def y_copy(k, i, slot, src, t):
        return pltpu.make_async_remote_copy(
            src_ref=s4.at[k, src], dst_ref=r4.at[k, slot], send_sem=c4s.at[k, i],
            recv_sem=c4r.at[k, slot], device_id={"y": t}, device_id_type=pl.DeviceIdType.MESH,
        )

    def z_copy(k, h, slot):
        return pltpu.make_async_remote_copy(
            src_ref=s5.at[k], dst_ref=r5.at[slot], send_sem=c5s.at[k, h], recv_sem=c5r.at[slot],
            device_id={"zl": k, "zh": h}, device_id_type=pl.DeviceIdType.MESH,
        )

    def z_first(k, h, slot):
        return pltpu.make_async_remote_copy(
            src_ref=s7.at[k, h], dst_ref=r7.at[slot], send_sem=c7s.at[k, h], recv_sem=c7r.at[slot],
            device_id={"zl": k, "zh": h}, device_id_type=pl.DeviceIdType.MESH,
        )

    def y_second(i, slot, t):
        return pltpu.make_async_remote_copy(
            src_ref=s8.at[t // 2], dst_ref=r8.at[slot], send_sem=c8s.at[i], recv_sem=c8r.at[slot],
            device_id={"y": t}, device_id_type=pl.DeviceIdType.MESH,
        )

    forward = pltpu.make_async_remote_copy(
        src_ref=mine, dst_ref=before, send_sem=fsem.at[0], recv_sem=fsem.at[1],
        device_id={"x": jnp.minimum(xx + 1, NX - 1)}, device_id_type=pl.DeviceIdType.MESH,
    )

    def summed(k, u):
        return gacc[k, co, u] + r1[k, u].astype(f32)

    def step_x1(k):
        send_core(k).wait_recv()
        s2[k, 0] = summed(k, partners(k)[0]).astype(bf16)
        s2[k, 1] = summed(k, second_of_first(k)).astype(bf16)
        send_x1(k).start()

    def step_x2(k):
        send_x1(k).wait_recv()
        s3[k] = (summed(k, partners(k)[1]) + r2[k, 1].astype(f32)).astype(bf16)
        send_x2(k).start()

    def step_y(k):
        send_x2(k).wait_recv()
        val = summed(k, xx) + r2[k, 0].astype(f32) + r3[k].astype(f32)
        bown[k, :, :8, :] = val[:64].reshape(NY, 8, LANES)
        rest = val[128:].reshape(NY // 2, 8, LANES)
        bown[k, : NY // 2, 8:, :] = rest
        bown[k, NY // 2 :, 8:, :] = rest
        s4[k] = bown[k].astype(bf16)
        for t in range(NY):
            for h in range(NZH):
                top = 64 + t * 8 + h * 4
                zown[k, h, t * 4 : t * 4 + 4, :] = val[top : top + 4]
        s7[k] = zown[k].astype(bf16)

        def go(i, c):
            t = (yy + i) % NY
            y_copy(k, i, yy, t, t).start()
            return c

        lax.fori_loop(1, NY, go, 0, unroll=True)
        for h in range(NZH):

            @pl.when(jnp.logical_or(zl != k, zh != h))
            def _():
                z_first(k, h, z12).start()

    def middle():
        def take(i, acc):
            t = (z12 + i) % NZ
            z_first(0, 0, t).wait_recv()
            return acc + r7[t].astype(f32)

        val = lax.fori_loop(1, NZ, take, zown[zl, zh], unroll=True).reshape(NY // 2, 8, LANES)
        mid[...] = val
        s8[...] = val.astype(bf16)

        def go(i, c):
            t = (yy + i) % NY
            y_second(i, yy, t).start()
            return c

        lax.fori_loop(1, NY, go, 0, unroll=True)

    def middle_end():
        def go(i, acc):
            t = (yy + i) % NY
            y_second(i, t, t).wait_recv()
            return acc + r8[t].astype(f32)

        return lax.fori_loop(1, NY, go, mid[yy // 2], unroll=True)

    def step_z(k):
        def go(i, acc):
            t = (yy + i) % NY
            y_copy(k, i, t, t, t).wait_recv()
            return acc + r4[k, t].astype(f32)

        val = lax.fori_loop(1, NY, go, bown[k, yy], unroll=True)
        cown[k] = val
        s5[k] = val.astype(bf16)
        for h in range(NZH):
            @pl.when(jnp.logical_or(zl != k, zh != h))
            def _():
                z_copy(k, h, z12).start()

    for k in ORDER:
        s1[k] = gacc[k, 1 - co].astype(bf16)
        send_core(k).start()

    mean_n = column(row2, 2)
    square_n = column(row2, 3)
    rstd_n = lax.rsqrt(square_n - mean_n * mean_n + EPS)
    affine_n = (zn[...] - mean_n) * rstd_n * gam[...] + bet[...]
    y_next = (affine_n * jax.nn.sigmoid(affine_n)).astype(bf16)
    y_out[0, 0] = y_next[:, :COLS]
    y_out[0, 1] = y_next[:, COLS:]

    for k in ORDER:
        step_x1(k)

    for step in range(len(ORDER) + 2):
        if step < 6:
            step_x2(ORDER[step])
        if step >= 2:
            step_y(ORDER[step - 2])
    for k in ORDER:
        step_z(k)
    middle()

    @pl.when(has_prev)
    def _():
        gz_next.wait_recv()

    @pl.when(jnp.logical_not(has_prev))
    def _():
        gzh[0] = jnp.zeros((CH, COLS), bf16)

    @pl.when(has_next)
    def _():
        gz_prev.wait_recv()

    @pl.when(jnp.logical_not(has_next))
    def _():
        gzh[1] = jnp.zeros((CH, COLS), bf16)

    put_shifts(gzs, 0, gzh[0])
    put_shifts(gzs, 1, gzo[0])
    put_shifts(gzs, 2, gzo[1])
    put_shifts(gzs, 3, gzh[1])
    zc[...] = jnp.zeros_like(zc)

    def back(t, c):
        a, b = t // 3, t % 3
        source = jnp.concatenate([gzs[2 - b, 2 - a, :CH], gzs[2 - b, 3 - a, :CH]], axis=1)
        zc[...] += dot(kv[a, b], source, TN)
        return c

    lax.fori_loop(0, 9, back, 0)
    grad_x = zc[...].astype(bf16)
    gx_out[0, 0] = grad_x[:, :COLS]
    gx_out[0, 1] = grad_x[:, COLS:]

    def gather_z(i, acc):
        t = (z12 + i) % NZ
        z_copy(0, 0, t).wait_recv()
        return acc + r5[t].astype(f32)

    total_z = lax.fori_loop(1, NZ, gather_z, cown[zl], unroll=True)
    mine[:8] = total_z[:8]
    mine[8:16] = middle_end()
    mine[16:] = total_z[8:]

    @pl.when(xx < NX - 1)
    def _():
        forward.start()

    @pl.when(has_next)
    def _():
        halos[0].wait_send()
        halos[2].wait_send()
        gz_next.wait_send()

    @pl.when(has_prev)
    def _():
        halos[1].wait_send()
        halos[3].wait_send()
        gz_prev.wait_send()

    sent_all(a_copy, ra, as_, ar, m, NM)
    sent_all(b_copy, rb, bs, br, yy, NY)
    sent_all(a_copy, ra2, as2, ar2, m, NM)
    sent_all(b_copy, rb2, bs2, br2, yy, NY)
    for k in range(NZL):
        send_core(k).wait_send()
        send_x1(k).wait_send()
        send_x2(k).wait_send()

        def sent_y(i, c):
            y_copy(k, i, yy, (yy + i) % NY, (yy + i) % NY).wait_send()
            return c

        lax.fori_loop(1, NY, sent_y, 0)
        for h in range(NZH):
            @pl.when(jnp.logical_or(zl != k, zh != h))
            def _():
                z_copy(k, h, z12).wait_send()
                z_first(k, h, z12).wait_send()

    def sent_second(i, c):
        y_second(i, yy, (yy + i) % NY).wait_send()
        return c

    lax.fori_loop(1, NY, sent_second, 0)
    gk_out[0] = mine[...]

    @pl.when(xx > 0)
    def _():
        forward.wait_recv()

    @pl.when(xx == 0)
    def _():
        before[...] = jnp.zeros_like(before)

    gk_out[1] = before[...]

    @pl.when(xx < NX - 1)
    def _():
        forward.wait_send()


def last(y_in, gx_in, raw, y_out, gx_out, gk_out, rows, sem):
    back = [
        pltpu.make_async_copy(y_in, y_out, sem.at[0]),
        pltpu.make_async_copy(gx_in, gx_out, sem.at[1]),
    ]
    for cp in back:
        cp.start()
    second, high = lax.axis_index("zh") == 1, lax.axis_index("y") >= NY // 2
    odd = lax.axis_index("y") % 2 == 1
    for i in range(2):
        tile = raw[i]
        rest = tile[16:]
        parts = (tile[:8], tile[8:16], jnp.where(high, pltpu.roll(rest, REST, 1), rest))
        for t, p in enumerate(parts):
            four = jnp.where(odd if t == 1 else second, p[4:], p[:4])
            lanes = slice(t * LANES, (t + 1) * LANES)
            if i == 0:
                rows[1:5, lanes] = four
            else:
                rows[0:1, lanes] = four[3:]
    share = 9 * CH * CH // (NH * NZH * NX)
    for v in range(NX):

        @pl.when(lax.axis_index("x") == v)
        def _():
            for start in range(0, share, LANES):
                n = min(LANES, share - start)
                r, col = divmod(share * v + start, CH)
                r = r - 4 * v + 1
                k = min(n, CH - col)
                piece = rows[r : r + 1, col : col + k]
                if k < n:
                    piece = jnp.concatenate([piece, rows[r + 1 : r + 2, : n - k]], axis=1)
                gk_out[pl.ds(start, n)] = piece.reshape(n)

    for cp in back:
        cp.wait()


def local(x_next, x_cur, grad_out, kernel, gamma, beta):
    vmem = pl.BlockSpec(memory_space=pltpu.VMEM)
    hbm = pl.BlockSpec(memory_space=pltpu.HBM)
    dma = pltpu.SemaphoreType.DMA
    V = pltpu.VMEM
    scratch = [
        V((CH,), f32), V((CH,), f32),
        V((4, CH, COLS), bf16), V((4, CH, COLS), bf16), V((2, CH, COLS), bf16),
        V((3, 3, CH, CH), bf16),
        V((3, 4, CH + REST, COLS), bf16), V((3, 4, 2 * REST, COLS), bf16), V((3, 4, CH, COLS), bf16),
        V((2, CH, COLS), bf16), V((2, CH, COLS), bf16), V((3, 4, CH, COLS), bf16),
        V((CH, 2 * COLS), f32), V((CH, 2 * COLS), f32), V((CH, 2 * COLS), f32), V((CH, 2 * COLS), f32),
        V((CH, COLS), f32), V((CH, 1), f32), V((CH, 1), f32),
        V((3, 32 * max(BLOCKS), CH), bf16),
        V((NM, 1, COLS), f32), V((NY, 1, COLS), f32), V((NM, 1, COLS), f32), V((NY, 1, COLS), f32),
        V((NZL, NC, NX, TALL, LANES), f32),
        V((NZL, NX, TALL, LANES), bf16), V((NZL, NX, TALL, LANES), bf16),
        V((NZL, 2, TALL, LANES), bf16), V((NZL, 2, TALL, LANES), bf16),
        V((NZL, TALL, LANES), bf16), V((NZL, TALL, LANES), bf16),
        V((NZL, NY, 16, LANES), bf16), V((NZL, NY, 16, LANES), bf16),
        V((NZL, NY, 16, LANES), f32),
        V((NZL, 16, LANES), bf16), V((NZL, 16, LANES), f32),
        V((NZ, 16, LANES), bf16),
        V((NZL, NZH, NY * 4, LANES), f32), V((NZL, NZH, NY * 4, LANES), bf16), V((NZ, NY * 4, LANES), bf16),
        V((NY // 2, 8, LANES), f32), V((NY // 2, 8, LANES), bf16), V((NY, 8, LANES), bf16),
        V((24, LANES), f32), V((24, LANES), f32),
        dma((6,)), dma((4,)), dma((4,)), dma((2,)), dma((2,)),
        dma((NM,)), dma((NM,)), dma((NY,)), dma((NY,)),
        dma((NM,)), dma((NM,)), dma((NY,)), dma((NY,)),
        dma((NZL,)), dma((NZL,)), dma((NZL,)), dma((NZL,)), dma((NZL,)), dma((NZL,)),
        dma((NZL, NY)), dma((NZL, NY)), dma((NZL, NZH)), dma((NZ,)),
        dma((NZL, NZH)), dma((NZ,)), dma((NY,)), dma((NY,)), dma((2,)),
    ]
    y_next, grad_x, quarters = pl.pallas_call(
        body,
        out_shape=(
            pltpu.VMEM(x_next.shape, bf16),
            pltpu.VMEM(x_next.shape, bf16),
            pltpu.VMEM((2, 24, LANES), f32),
        ),
        in_specs=[hbm] * 6,
        out_specs=(vmem, vmem, vmem),
        scratch_shapes=scratch,
        compiler_params=pltpu.CompilerParams(
            collective_id=0, has_side_effects=True, vmem_limit_bytes=40 * 1024 * 1024
        ),
    )(*(pltpu.with_memory_space_constraint(v, pltpu.HBM) for v in (x_next, x_cur, grad_out, kernel, gamma, beta)))
    return pl.pallas_call(
        last,
        out_shape=(
            jax.ShapeDtypeStruct(x_next.shape, bf16),
            jax.ShapeDtypeStruct(x_next.shape, bf16),
            jax.ShapeDtypeStruct((9 * CH * CH // (NH * NZH * NX),), f32),
        ),
        in_specs=[vmem, vmem, vmem],
        out_specs=(hbm, hbm, vmem),
        scratch_shapes=[V((8, 3 * LANES), f32), dma((2,))],
        compiler_params=pltpu.CompilerParams(vmem_limit_bytes=8 * 1024 * 1024),
    )(y_next, grad_x, quarters)


def solution(mesh):
    torus = Mesh(mesh.devices.reshape(NY, NZL, NC, NZH, NX), HEIGHT + DP)
    image = P(DP, HEIGHT, None, None)
    return jax.shard_map(
        local,
        mesh=torus,
        in_specs=(image, image, image, P(), P(), P()),
        out_specs=(image, image, P(HEIGHT + DP)),
        check_vma=False,
    )
```
